768 devices in a mesh: seq: 24 (over y, z_hi), mp: 32 (over z_lo, x, core).
Axes of the slice: x: 4, y: 8, z: 12 (z_hi: 3, z_lo: 4; z = z_hi * 4 + z_lo), core: 2. Of those that a mesh axis runs over, the one named last changes fastest.
Arguments:
- tokens: bfloat16 [3072, 4096], P('seq', 'mp'), may hold values from -68 to 68
- w_qkv: bfloat16 [3, 4096, 4096], P(None, None, 'mp'), may hold values from -0.09375 to 0.09375
- w_pos: bfloat16 [4096, 4096], P(None, 'mp'), may hold values from -0.09375 to 0.09375
- w_out: bfloat16 [4096, 4096], P('mp'), may hold values from -0.09375 to 0.09375
- content_bias: float32 [32, 128], P('mp'), may hold values from -4 to 4
- position_bias: float32 [32, 128], P('mp'), may hold values from -4 to 4
- doc_ids: int32 [3072], P('seq'), may hold values from 0 to 23, never falling along the last dimension, each value on 1 to 256 neighbouring positions
Outputs:
- attn_out: bfloat16 [3072, 4096], P('seq', 'mp')
The draws below stay inside these ranges and needn't reach their ends.
All inputs are finite; a program needn't handle non-finite values.
Results may differ from the reference program's by a relative error of at most 0.0067.
Values may be sent and summed in bfloat16 or wider, within the bound.
A program may use at most 32 MiB of HBM per device.

```python
import math
import jax
import jax.numpy as jnp
import numpy as np
from jax import lax

D = 4096
HEADS = 32
HEAD_DIM = 128
SEG = 128
TOKENS = 3072


def draw_tokens(key, part):
    first = jax.random.fold_in(key, 0)
    values = jnp.clip(jax.random.normal(first, (TOKENS, D), jnp.float32), -6.0, 6.0)
    return values.astype(jnp.bfloat16)


def block_levels(rng, shape, cuts, smallest, largest):
    gain = 1.0
    for dim, parts in cuts:
        steps = jax.random.uniform(jax.random.fold_in(jax.random.fold_in(rng, 6), dim), (parts,), jnp.float32, smallest / len(cuts), largest / len(cuts))
        gain = gain * jnp.repeat(jnp.exp(steps), shape[dim] // parts).reshape((-1,) + (1,) * (len(shape) - 1 - dim))
    return gain


def length_profile(count, total, most, skew):
    weights = [(1 << 20) // math.isqrt(rank ** skew) + 1 for rank in range(2, count + 1)]
    spare, given = total - most - (count - 1), [1] * (count - 1)
    while spare > 0:
        movable = [i for i in range(count - 1) if given[i] < most]
        mass, remaining = sum([weights[i] for i in movable]), spare
        for i in movable:
            addition = min(most - given[i], max(1, remaining * weights[i] // mass), spare)
            given[i] = given[i] + addition
            spare = spare - addition
    return np.array([most] + given)


def uneven_parts(stream_key, amount, total, bound, skew):
    if amount == 2:
        one = jax.random.randint(stream_key, (), max(1, total - bound), min(bound, total - 1) + 1)
        return jnp.stack([one, total - one])
    lengths = jnp.asarray(length_profile(amount, total, bound, skew), jnp.int32)
    twos = (amount - 1) // 2
    source_of, taker = lengths[1:1 + 2 * twos:2], lengths[2:2 + 2 * twos:2]
    slack = jnp.minimum(source_of - 1, bound - taker)
    moved = jax.random.randint(jax.random.fold_in(stream_key, 1), (twos,), 0, 1 << 20) % (slack + 1)
    lengths = lengths.at[1:1 + 2 * twos:2].set(source_of - moved).at[2:2 + 2 * twos:2].set(taker + moved)
    return lengths[jax.random.permutation(jax.random.fold_in(stream_key, 2), amount)]


def normal_values(rng, extent, scale, most, cuts=(), kind=jnp.bfloat16):
    values = jax.random.normal(rng, extent, jnp.float32) * scale
    if len(cuts) > 0:
        values = block_levels(rng, extent, cuts, -0.22, 0.18) * values
    return jnp.clip(values, min=-most, max=most).astype(kind)


def setup_inputs(seed: int = 0) -> dict:
    key_list = jax.random.split(jax.random.key(seed), 8)
    tokens = draw_tokens(jax.random.fold_in(key_list[7], 71), 0)
    w_qkv = normal_values(key_list[1], (3, D, D), D ** -0.5, 0.09375, ((2, 32),))
    w_pos = normal_values(key_list[2], (D, D), D ** -0.5, 0.09375, ((1, 32),))
    w_out = normal_values(key_list[3], (D, D), D ** -0.5, 0.09375, ((0, 32),))
    content_bias = normal_values(key_list[4], (HEADS, HEAD_DIM), 1.0, 4.0, ((0, 32),), jnp.float32)
    position_bias = normal_values(key_list[5], (HEADS, HEAD_DIM), 1.0, 4.0, ((0, 32),), jnp.float32)
    doc_ids = jnp.searchsorted(jnp.cumsum(uneven_parts(key_list[6], TOKENS // SEG, TOKENS, 2 * SEG, 1)), jnp.arange(TOKENS), side="right").astype(jnp.int32)
    return dict(tokens=tokens, w_qkv=w_qkv, w_pos=w_pos, w_out=w_out, content_bias=content_bias, position_bias=position_bias, doc_ids=doc_ids)


def sinus_table(count, width):
    place = jnp.arange(count, dtype=jnp.float32)[:, None]
    freqs = 1.0 / 10000.0 ** (jnp.arange(0, width, 2, dtype=jnp.float32) / width)
    angle = place * freqs[None, :]
    return jnp.concatenate([jnp.sin(angle), jnp.cos(angle)], axis=1).astype(jnp.bfloat16)

def attend(query_content, query_pos, keys, values, rel_keys, allowed, heads_here, head_dim):
    rows = query_content.shape[0]
    span = keys.shape[0]
    qc_heads = query_content.reshape(rows, heads_here, head_dim).astype(jnp.float32)
    qp_heads = query_pos.reshape(rows, heads_here, head_dim).astype(jnp.float32)
    key_heads = keys.reshape(span, heads_here, head_dim).astype(jnp.float32)
    val_heads = values.reshape(span, heads_here, head_dim).astype(jnp.float32)
    rel_heads = rel_keys.reshape(span, heads_here, head_dim).astype(jnp.float32)
    content = jnp.einsum('ihd,jhd->hij', qc_heads, key_heads)
    pos_full = jnp.einsum('ihd,rhd->hir', qp_heads, rel_heads)
    offset = jnp.arange(rows, dtype=jnp.int32)[:, None] + span // 2 - jnp.arange(span, dtype=jnp.int32)[None, :]
    offset = jnp.clip(offset, 0, span - 1)
    pos = jnp.take_along_axis(pos_full, jnp.broadcast_to(offset[None], pos_full.shape), axis=2)
    score = (content + pos) * (1.0 / jnp.sqrt(jnp.float32(head_dim)))
    score = jnp.where(allowed[None], score, jnp.float32(-1e+30))
    top = lax.optimization_barrier(jnp.max(score, axis=2, keepdims=True))
    expo = jnp.where(allowed[None], jnp.exp(score - top), jnp.float32(0.0))
    weights = (expo / lax.optimization_barrier(jnp.sum(expo, axis=2, keepdims=True))).astype(jnp.bfloat16)
    out = jnp.einsum('hij,jhd->ihd', weights.astype(jnp.float32), val_heads)
    return out.astype(jnp.bfloat16).reshape(rows, heads_here * head_dim)

def reference(tokens, w_qkv, w_pos, w_out, content_bias, position_bias, doc_ids):
    query = jnp.dot(tokens, w_qkv[0], preferred_element_type=jnp.float32)
    query_content = (query + content_bias.reshape(D)[None, :]).astype(jnp.bfloat16)
    query_pos = (query + position_bias.reshape(D)[None, :]).astype(jnp.bfloat16)
    key_rows = jnp.dot(tokens, w_qkv[1], preferred_element_type=jnp.float32).astype(jnp.bfloat16)
    value_rows = jnp.dot(tokens, w_qkv[2], preferred_element_type=jnp.float32).astype(jnp.bfloat16)
    rel_keys = jnp.dot(sinus_table(2 * SEG, D), w_pos, preferred_element_type=jnp.float32).astype(jnp.bfloat16)
    key_padded = jnp.concatenate([jnp.zeros((SEG, D), jnp.bfloat16), key_rows], axis=0)
    value_padded = jnp.concatenate([jnp.zeros((SEG, D), jnp.bfloat16), value_rows], axis=0)
    doc_padded = jnp.concatenate([jnp.full((SEG,), -1, jnp.int32), doc_ids.astype(jnp.int32)], axis=0)
    reach = jnp.arange(2 * SEG, dtype=jnp.int32)[None, :] <= jnp.arange(SEG, dtype=jnp.int32)[:, None] + SEG

    def one_segment(segment):
        start = (segment * SEG).astype(jnp.int32)
        keys = lax.dynamic_slice_in_dim(key_padded, start, 2 * SEG, 0)
        values = lax.dynamic_slice_in_dim(value_padded, start, 2 * SEG, 0)
        key_doc = lax.dynamic_slice_in_dim(doc_padded, start, 2 * SEG, 0)
        own_doc = lax.dynamic_slice_in_dim(doc_ids.astype(jnp.int32), start, SEG, 0)
        qc_rows = lax.dynamic_slice_in_dim(query_content, start, SEG, 0)
        qp_rows = lax.dynamic_slice_in_dim(query_pos, start, SEG, 0)
        allowed = reach & (key_doc[None, :] == own_doc[:, None])
        return attend(qc_rows, qp_rows, keys, values, rel_keys, allowed, HEADS, HEAD_DIM)
    head_out = lax.map(one_segment, jnp.arange(TOKENS // SEG, dtype=jnp.int32))
    head_out = head_out.reshape(TOKENS, D)
    return jnp.dot(head_out, w_out, preferred_element_type=jnp.float32).astype(jnp.bfloat16)
```

```python
import jax
import jax.numpy as jnp
import numpy as np
from jax import lax
from jax.experimental import pallas as pl
from jax.experimental.pallas import tpu as pltpu
from jax.sharding import PartitionSpec as P

MESH = pl.DeviceIdType.MESH
F32 = jnp.float32
BF16 = jnp.bfloat16


def sinus_reversed(count, width):
    place = np.arange(count, dtype=np.float32)[::-1, None]
    freqs = np.float32(1.0) / np.power(
        np.float32(10000.0), np.arange(0, width, 2, dtype=np.float32) / np.float32(width)
    )
    angle = place * freqs[None, :].astype(np.float32)
    table = np.concatenate([np.sin(angle), np.cos(angle)], axis=1)
    return table.astype(jnp.bfloat16)


def dot(a, b):
    return jnp.dot(a, b, preferred_element_type=F32)


def dot_t(a, b):
    return lax.dot_general(a, b, (((1,), (1,)), ((), ())), preferred_element_type=F32)


def kernel(
    tok, wqkv, wpos, wout, cbias, pbias, doc, sinus, out,
    toks, wv, wp, sn, wo, acc, kvs, kvm, docm, ho, part, rcv,
    lsem, tok_ss, tok_rs, w_ss, w_rs, kv_ss, kv_rs, ho_ss, ho_rs, p_ss, p_rs,
):
    seq = lax.axis_index("seq")
    me = lax.axis_index("mp")
    n_seq = lax.axis_size("seq")
    z, x, c = me // 8, (me // 2) % 4, me % 2
    xc = me % 8
    nxt, prv = (seq + 1) % n_seq, (seq + n_seq - 1) % n_seq
    xr, xl = (x + 1) % 4, (x + 3) % 4
    dirn = 1 - 2 * c
    x_up, x_dn = (x - dirn + 4) % 4, (x + dirn + 4) % 4
    x_far = (x + 2) % 4
    inner = (z // 2 + z % 2) % 2
    za, zb, zc = z + 1 - 2 * (z % 2), 3 - z, (z + 2) % 4
    zo = [z, za, inner * zb + (1 - inner) * zc, inner * zc + (1 - inner) * zb]

    def mp_of(zz, xx, cc):
        return (zz * 4 + xx) * 2 + cc

    barrier = pltpu.get_barrier_semaphore()
    for k in range(1, 8):
        pl.semaphore_signal(
            barrier, inc=1, device_id={"mp": z * 8 + (xc + k) % 8}, device_id_type=MESH
        )
    for k in range(1, 4):
        pl.semaphore_signal(
            barrier, inc=1, device_id={"mp": mp_of(zo[k], x, c)}, device_id_type=MESH
        )
    pl.semaphore_signal(barrier, inc=1, device_id={"seq": nxt}, device_id_type=MESH)
    pl.semaphore_signal(barrier, inc=1, device_id={"seq": prv}, device_id_type=MESH)

    ld_sn = pltpu.make_async_copy(sinus, sn, lsem.at[0])
    ld_wp = pltpu.make_async_copy(wpos, wp, lsem.at[1])
    ld_wv = pltpu.make_async_copy(wqkv, wv, lsem.at[2])
    ld_sn.start()
    ld_wp.start()
    ld_wv.start()
    toks[me] = tok[...]

    pl.semaphore_wait(barrier, 12)

    sends = []

    def push(src, slot, target):
        n = len(sends)
        copy = pltpu.make_async_remote_copy(
            src_ref=src,
            dst_ref=toks.at[slot],
            send_sem=tok_ss.at[n],
            recv_sem=tok_rs.at[slot],
            device_id={"mp": target},
            device_id_type=MESH,
        )
        copy.start()
        sends.append(copy)

    def landed(slot):
        pltpu.make_async_remote_copy(
            src_ref=tok,
            dst_ref=toks.at[slot],
            send_sem=tok_ss.at[0],
            recv_sem=tok_rs.at[slot],
            device_id={"mp": me},
            device_id_type=MESH,
        ).wait_recv()

    push(tok, me, mp_of(zo[1], x, c))
    push(tok, me, mp_of(z, xr, c))
    push(tok, me, mp_of(z, xl, c))
    push(tok, me, mp_of(zo[2], x, c))
    push(tok, me, mp_of(zo[3], x, c))
    push(tok, me, mp_of(z, x, 1 - c))
    doc_copy = pltpu.make_async_remote_copy(
        src_ref=doc,
        dst_ref=docm,
        send_sem=kv_ss.at[2],
        recv_sem=kv_rs.at[2],
        device_id={"seq": nxt},
        device_id_type=MESH,
    )
    doc_copy.start()

    ld_sn.wait()
    ld_wp.wait()
    rel = dot(sn[...], wp[...]).astype(BF16)

    def from_z(k):
        slot = mp_of(zo[k], x, c)
        landed(slot)
        push(toks.at[slot], slot, mp_of(z, xr, c))
        push(toks.at[slot], slot, mp_of(z, xl, c))
        push(toks.at[slot], slot, mp_of(z, x, 1 - c))

    def from_x(k):
        slot = mp_of(zo[k], x_up, c)
        landed(slot)
        push(toks.at[slot], slot, mp_of(z, x_dn, c))
        push(toks.at[slot], slot, mp_of(z, x, 1 - c))
        slot = mp_of(zo[k], x_dn, c)
        landed(slot)
        push(toks.at[slot], slot, mp_of(z, x, 1 - c))

    def from_far(k):
        slot = mp_of(zo[k], x_far, c)
        landed(slot)
        push(toks.at[slot], slot, mp_of(z, x, 1 - c))

    def from_core(k):
        for xx in (x, x_up, x_dn, x_far):
            landed(mp_of(zo[k], xx, 1 - c))

    def project(k):
        zz = zo[k]
        left = jnp.concatenate([toks[zz * 8 + j] for j in range(8)], axis=1)
        rows = pl.ds(pl.multiple_of(zz * 1024, 1024), 1024)
        right = jnp.concatenate([wv[0, rows, :], wv[1, rows, :], wv[2, rows, :]], axis=1)
        term = dot(left, right)
        if k == 0:
            acc[...] = term
        else:
            acc[...] += term

    from_z(1)
    from_x(0)
    from_z(2)
    from_x(1)
    from_z(3)
    from_far(0)
    from_x(2)
    ld_wv.wait()
    from_core(0)
    project(0)
    from_far(1)
    from_x(3)
    from_core(1)
    project(1)
    from_far(2)
    from_far(3)

    w_copies = []
    for k in (1, 7, 2, 6, 3, 5, 4):
        to = (xc + k) % 8
        for zz in range(4):
            cols = pl.ds(pl.multiple_of((zz * 8 + to) * 128, 128), 128)
            pltpu.make_async_remote_copy(
                src_ref=wout.at[:, cols],
                dst_ref=wo.at[xc, zz],
                send_sem=w_ss.at[k],
                recv_sem=w_rs.at[xc],
                device_id={"mp": z * 8 + to},
                device_id_type=MESH,
            ).start()
    for zz in range(4):
        cols = pl.ds(pl.multiple_of((zz * 8 + xc) * 128, 128), 128)
        pltpu.make_async_copy(wout.at[:, cols], wo.at[xc, zz], lsem.at[3]).start()

    from_core(2)
    project(2)
    from_core(3)
    project(3)

    kvs[0] = acc[:, 128:256].astype(BF16)
    kvs[1] = acc[:, 256:384].astype(BF16)
    kv_copies = []
    for i in range(2):
        copy = pltpu.make_async_remote_copy(
            src_ref=kvs.at[i],
            dst_ref=kvm.at[i],
            send_sem=kv_ss.at[i],
            recv_sem=kv_rs.at[i],
            device_id={"seq": nxt},
            device_id_type=MESH,
        )
        copy.start()
        kv_copies.append(copy)

    query = acc[:, 0:128]
    qc = (query + cbias[...]).astype(BF16)
    qp = (query + pbias[...]).astype(BF16)
    pos = pltpu.roll(dot_t(qp, rel), 129, 1, stride=1, stride_axis=0)
    scale = F32(1.0) / jnp.sqrt(F32(128.0))
    own_doc = doc[...]
    row_doc = jnp.transpose(jnp.broadcast_to(own_doc, (128, 128)))
    rows = lax.broadcasted_iota(jnp.int32, (128, 128), 0)
    cols = lax.broadcasted_iota(jnp.int32, (128, 128), 1)
    ok_own = (cols <= rows) & (row_doc == own_doc)
    s_own = (dot_t(qc, kvs[0]) + pos[:, 128:256]) * scale
    s_own = jnp.where(ok_own, s_own, F32(-1e30))
    top_own = jnp.max(s_own, axis=1, keepdims=True)

    doc_copy.wait_recv()
    ok_mem = (row_doc == docm[...]) & (seq > 0)
    kv_copies[0].wait_recv()
    s_mem = (dot_t(qc, kvm[0]) + pos[:, 0:128]) * scale
    s_mem = jnp.where(ok_mem, s_mem, F32(-1e30))
    top = jnp.maximum(top_own, jnp.max(s_mem, axis=1, keepdims=True))
    e_own = jnp.where(ok_own, jnp.exp(s_own - top), F32(0.0))
    e_mem = jnp.where(ok_mem, jnp.exp(s_mem - top), F32(0.0))
    total = jnp.sum(e_own, axis=1, keepdims=True) + jnp.sum(e_mem, axis=1, keepdims=True)
    w_own = (e_own / total).astype(BF16)
    w_mem = (e_mem / total).astype(BF16)
    kv_copies[1].wait_recv()
    head = dot(w_own, kvs[1]) + dot(w_mem, kvm[1])
    ho[xc] = head.astype(BF16)

    ho_copies = []
    for k in (1, 7, 2, 6, 3, 5, 4):
        copy = pltpu.make_async_remote_copy(
            src_ref=ho.at[xc],
            dst_ref=ho.at[xc],
            send_sem=ho_ss.at[k],
            recv_sem=ho_rs.at[xc],
            device_id={"mp": z * 8 + (xc + k) % 8},
            device_id_type=MESH,
        )
        copy.start()
        ho_copies.append(copy)

    for k in range(1, 8):
        slot = (xc + k) % 8
        pltpu.make_async_remote_copy(
            src_ref=wo.at[slot],
            dst_ref=wo.at[slot],
            send_sem=w_ss.at[0],
            recv_sem=w_rs.at[slot],
            device_id={"mp": me},
            device_id_type=MESH,
        ).wait_recv()
    pltpu.make_async_copy(wo.at[xc], wo.at[xc], lsem.at[3]).wait()
    for k in range(1, 8):
        slot = (xc + k) % 8
        pltpu.make_async_remote_copy(
            src_ref=ho.at[slot],
            dst_ref=ho.at[slot],
            send_sem=ho_ss.at[0],
            recv_sem=ho_rs.at[slot],
            device_id={"mp": me},
            device_id_type=MESH,
        ).wait_recv()

    heads = jnp.concatenate([ho[j] for j in range(8)], axis=1)
    p_copies = []
    for k in (3, 2, 1, 0):
        zz = zo[k]
        right = jnp.concatenate([wo[j, zz] for j in range(8)], axis=0)
        part[zz] = dot(heads, right)
        if k > 0:
            copy = pltpu.make_async_remote_copy(
                src_ref=part.at[zz],
                dst_ref=rcv.at[z],
                send_sem=p_ss.at[k],
                recv_sem=p_rs.at[z],
                device_id={"mp": mp_of(zz, x, c)},
                device_id_type=MESH,
            )
            copy.start()
            p_copies.append(copy)
    result = part[z]
    for k in (1, 2, 3):
        zz = zo[k]
        pltpu.make_async_remote_copy(
            src_ref=rcv.at[zz],
            dst_ref=rcv.at[zz],
            send_sem=p_ss.at[0],
            recv_sem=p_rs.at[zz],
            device_id={"mp": me},
            device_id_type=MESH,
        ).wait_recv()
        result = result + rcv[zz]
    out[...] = result.astype(BF16)

    for copy in sends:
        copy.wait_send()
    for k in range(1, 8):
        pltpu.make_async_remote_copy(
            src_ref=wo.at[xc],
            dst_ref=wo.at[xc],
            send_sem=w_ss.at[k],
            recv_sem=w_rs.at[xc],
            device_id={"mp": me},
            device_id_type=MESH,
        ).wait_send()
    for copy in kv_copies + [doc_copy] + ho_copies + p_copies:
        copy.wait_send()


def shards(tokens, w_qkv, w_pos, w_out, content_bias, position_bias, doc_ids):
    vmem = pl.BlockSpec(memory_space=pltpu.VMEM)
    hbm = pl.BlockSpec(memory_space=pl.ANY)
    sinus = jnp.asarray(sinus_reversed(256, 4096))
    return pl.pallas_call(
        kernel,
        out_shape=jax.ShapeDtypeStruct((128, 128), BF16),
        in_specs=[vmem, hbm, hbm, hbm, vmem, vmem, vmem, hbm],
        out_specs=vmem,
        scratch_shapes=[
            pltpu.VMEM((32, 128, 128), BF16),
            pltpu.VMEM((3, 4096, 128), BF16),
            pltpu.VMEM((4096, 128), BF16),
            pltpu.VMEM((256, 4096), BF16),
            pltpu.VMEM((8, 4, 128, 128), BF16),
            pltpu.VMEM((128, 384), F32),
            pltpu.VMEM((2, 128, 128), BF16),
            pltpu.VMEM((2, 128, 128), BF16),
            pltpu.VMEM((1, 128), jnp.int32),
            pltpu.VMEM((8, 128, 128), BF16),
            pltpu.VMEM((4, 128, 128), F32),
            pltpu.VMEM((4, 128, 128), F32),
            pltpu.SemaphoreType.DMA((4,)),
            pltpu.SemaphoreType.DMA((31,)),
            pltpu.SemaphoreType.DMA((32,)),
            pltpu.SemaphoreType.DMA((8,)),
            pltpu.SemaphoreType.DMA((8,)),
            pltpu.SemaphoreType.DMA((3,)),
            pltpu.SemaphoreType.DMA((3,)),
            pltpu.SemaphoreType.DMA((8,)),
            pltpu.SemaphoreType.DMA((8,)),
            pltpu.SemaphoreType.DMA((4,)),
            pltpu.SemaphoreType.DMA((4,)),
        ],
        compiler_params=pltpu.CompilerParams(
            collective_id=0, has_side_effects=True, vmem_limit_bytes=60000 * 1024
        ),
        name="layer",
    )(tokens, w_qkv, w_pos, w_out, content_bias, position_bias, doc_ids.reshape(1, 128), sinus)


def solution(mesh):
    in_specs = (
        P("seq", "mp"),
        P(None, None, "mp"),
        P(None, "mp"),
        P("mp", None),
        P("mp", None),
        P("mp", None),
        P("seq"),
    )
    out_specs = P("seq", "mp")
    return jax.shard_map(shards, mesh=mesh, in_specs=in_specs, out_specs=out_specs, check_vma=False)
```

```python
import jax
import jax.numpy as jnp
import numpy as np
from jax import lax
from jax.experimental import pallas as pl
from jax.experimental.pallas import tpu as pltpu
from jax.sharding import PartitionSpec as P

MESH = pl.DeviceIdType.MESH
F32 = jnp.float32
BF16 = jnp.bfloat16


def sinus_reversed(count, width):
    place = np.arange(count, dtype=np.float32)[::-1, None]
    freqs = np.float32(1.0) / np.power(
        np.float32(10000.0), np.arange(0, width, 2, dtype=np.float32) / np.float32(width)
    )
    angle = place * freqs[None, :].astype(np.float32)
    table = np.concatenate([np.sin(angle), np.cos(angle)], axis=1)
    return table.astype(jnp.bfloat16)


def dot(a, b):
    return jnp.dot(a, b, preferred_element_type=F32)


def dot_t(a, b):
    return lax.dot_general(a, b, (((1,), (1,)), ((), ())), preferred_element_type=F32)


def kernel(
    tok_in, wqkv, wpos, wout, cbias_in, pbias_in, doc_in, sinus, out,
    cbias, pbias, doc, toks, wv, wp, sn, wo, acc, kvs, kvm, docm, ho, part, rcv,
    lsem, tok_ss, tok_rs, w_ss, w_rs, kv_ss, kv_rs, ho_ss, ho_rs, p_ss, p_rs,
):
    seq = lax.axis_index("seq")
    me = lax.axis_index("mp")
    n_seq = lax.axis_size("seq")
    z, x, c = me // 8, (me // 2) % 4, me % 2
    xc = me % 8
    nxt, prv = (seq + 1) % n_seq, (seq + n_seq - 1) % n_seq
    xr, xl = (x + 1) % 4, (x + 3) % 4
    dirn = 1 - 2 * c
    x_up, x_dn = (x - dirn + 4) % 4, (x + dirn + 4) % 4
    x_far = (x + 2) % 4
    inner = (z // 2 + z % 2) % 2
    za, zb, zc = z + 1 - 2 * (z % 2), 3 - z, (z + 2) % 4
    zo = [z, za, inner * zb + (1 - inner) * zc, inner * zc + (1 - inner) * zb]

    def mp_of(zz, xx, cc):
        return (zz * 4 + xx) * 2 + cc

    barrier = pltpu.get_barrier_semaphore()
    for k in range(1, 8):
        pl.semaphore_signal(
            barrier, inc=1, device_id={"mp": z * 8 + (xc + k) % 8}, device_id_type=MESH
        )
    for k in range(1, 4):
        pl.semaphore_signal(
            barrier, inc=1, device_id={"mp": mp_of(zo[k], x, c)}, device_id_type=MESH
        )
    pl.semaphore_signal(barrier, inc=1, device_id={"seq": prv}, device_id_type=MESH)

    ld_tok = pltpu.make_async_copy(tok_in, toks.at[me], lsem.at[4])
    ld_tok.start()
    ld_doc = pltpu.make_async_copy(doc_in, doc, lsem.at[5])
    ld_doc.start()
    ld_cb = pltpu.make_async_copy(cbias_in, cbias, lsem.at[6])
    ld_cb.start()
    ld_pb = pltpu.make_async_copy(pbias_in, pbias, lsem.at[7])
    ld_pb.start()
    ld_sn = pltpu.make_async_copy(sinus, sn, lsem.at[0])
    ld_wp = pltpu.make_async_copy(wpos, wp, lsem.at[1])
    ld_wv = pltpu.make_async_copy(wqkv, wv, lsem.at[2])
    ld_sn.start()
    ld_wp.start()
    ld_wv.start()
    tok = toks.at[me]
    ld_tok.wait()
    ld_doc.wait()

    pl.semaphore_wait(barrier, 11)

    sends = []

    def push(src, slot, target):
        n = len(sends)
        copy = pltpu.make_async_remote_copy(
            src_ref=src,
            dst_ref=toks.at[slot],
            send_sem=tok_ss.at[n],
            recv_sem=tok_rs.at[slot],
            device_id={"mp": target},
            device_id_type=MESH,
        )
        copy.start()
        sends.append(copy)

    def landed(slot):
        pltpu.make_async_remote_copy(
            src_ref=tok,
            dst_ref=toks.at[slot],
            send_sem=tok_ss.at[0],
            recv_sem=tok_rs.at[slot],
            device_id={"mp": me},
            device_id_type=MESH,
        ).wait_recv()

    push(tok, me, mp_of(zo[1], x, c))
    push(tok, me, mp_of(z, xr, c))
    push(tok, me, mp_of(z, xl, c))
    push(tok, me, mp_of(zo[2], x, c))
    push(tok, me, mp_of(zo[3], x, c))
    push(tok, me, mp_of(z, x, 1 - c))
    doc_copy = pltpu.make_async_remote_copy(
        src_ref=doc,
        dst_ref=docm,
        send_sem=kv_ss.at[2],
        recv_sem=kv_rs.at[2],
        device_id={"seq": nxt},
        device_id_type=MESH,
    )
    doc_copy.start()

    ld_sn.wait()
    ld_wp.wait()
    rel = dot(sn[...], wp[...]).astype(BF16)

    def from_z(k):
        slot = mp_of(zo[k], x, c)
        landed(slot)
        push(toks.at[slot], slot, mp_of(z, xr, c))
        push(toks.at[slot], slot, mp_of(z, xl, c))
        if k == 3:
            push(toks.at[slot], slot, mp_of(z, x_far, c))
        push(toks.at[slot], slot, mp_of(z, x, 1 - c))

    def from_x(k):
        slot = mp_of(zo[k], x_up, c)
        landed(slot)
        if k < 3:
            push(toks.at[slot], slot, mp_of(z, x_dn, c))
        push(toks.at[slot], slot, mp_of(z, x, 1 - c))
        slot = mp_of(zo[k], x_dn, c)
        landed(slot)
        push(toks.at[slot], slot, mp_of(z, x, 1 - c))

    def from_far(k):
        slot = mp_of(zo[k], x_far, c)
        landed(slot)
        push(toks.at[slot], slot, mp_of(z, x, 1 - c))

    def from_core(k):
        for xx in (x, x_up, x_dn, x_far):
            landed(mp_of(zo[k], xx, 1 - c))

    def project(k):
        zz = zo[k]
        left = jnp.concatenate([toks[zz * 8 + j] for j in range(8)], axis=1)
        rows = pl.ds(pl.multiple_of(zz * 1024, 1024), 1024)
        right = jnp.concatenate([wv[0, rows, :], wv[1, rows, :], wv[2, rows, :]], axis=1)
        term = dot(left, right)
        if k == 0:
            acc[...] = term
        else:
            acc[...] += term

    for k in (1, 2, 3):
        from_z(k)
    for k in (0, 1, 2, 3):
        from_x(k)
    for k in (0, 1, 2, 3):
        from_far(k)

    w_copies = []
    for k in (1, 7, 2, 6, 3, 5, 4):
        to = (xc + k) % 8
        for zz in range(4):
            cols = pl.ds(pl.multiple_of((zz * 8 + to) * 128, 128), 128)
            pltpu.make_async_remote_copy(
                src_ref=wout.at[:, cols],
                dst_ref=wo.at[xc, zz],
                send_sem=w_ss.at[k],
                recv_sem=w_rs.at[xc],
                device_id={"mp": z * 8 + to},
                device_id_type=MESH,
            ).start()
    for zz in range(4):
        cols = pl.ds(pl.multiple_of((zz * 8 + xc) * 128, 128), 128)
        pltpu.make_async_copy(wout.at[:, cols], wo.at[xc, zz], lsem.at[3]).start()

    ld_wv.wait()
    for k in (0, 1, 2, 3):
        from_core(k)
        project(k)

    kvs[0] = acc[:, 128:256].astype(BF16)
    kvs[1] = acc[:, 256:384].astype(BF16)
    kv_copies = []
    for i in range(2):
        copy = pltpu.make_async_remote_copy(
            src_ref=kvs.at[i],
            dst_ref=kvm.at[i],
            send_sem=kv_ss.at[i],
            recv_sem=kv_rs.at[i],
            device_id={"seq": nxt},
            device_id_type=MESH,
        )
        copy.start()
        kv_copies.append(copy)

    ld_cb.wait()
    ld_pb.wait()
    query = acc[:, 0:128]
    qc = (query + cbias[...]).astype(BF16)
    qp = (query + pbias[...]).astype(BF16)
    pos = pltpu.roll(dot_t(qp, rel), 129, 1, stride=1, stride_axis=0)
    scale = F32(1.0) / jnp.sqrt(F32(128.0))
    own_doc = doc[...]
    row_doc = jnp.transpose(jnp.broadcast_to(own_doc, (128, 128)))
    rows = lax.broadcasted_iota(jnp.int32, (128, 128), 0)
    cols = lax.broadcasted_iota(jnp.int32, (128, 128), 1)
    ok_own = (cols <= rows) & (row_doc == own_doc)
    s_own = (dot_t(qc, kvs[0]) + pos[:, 128:256]) * scale
    s_own = jnp.where(ok_own, s_own, F32(-1e30))
    top_own = jnp.max(s_own, axis=1, keepdims=True)

    doc_copy.wait_recv()
    ok_mem = (row_doc == docm[...]) & (seq > 0)
    kv_copies[0].wait_recv()
    s_mem = (dot_t(qc, kvm[0]) + pos[:, 0:128]) * scale
    s_mem = jnp.where(ok_mem, s_mem, F32(-1e30))
    top = jnp.maximum(top_own, jnp.max(s_mem, axis=1, keepdims=True))
    e_own = jnp.where(ok_own, jnp.exp(s_own - top), F32(0.0))
    e_mem = jnp.where(ok_mem, jnp.exp(s_mem - top), F32(0.0))
    total = jnp.sum(e_own, axis=1, keepdims=True) + jnp.sum(e_mem, axis=1, keepdims=True)
    w_own = (e_own / total).astype(BF16)
    w_mem = (e_mem / total).astype(BF16)
    kv_copies[1].wait_recv()
    head = dot(w_own, kvs[1]) + dot(w_mem, kvm[1])
    ho[xc] = head.astype(BF16)

    ho_copies = []
    for k in (1, 7, 2, 6, 3, 5, 4):
        copy = pltpu.make_async_remote_copy(
            src_ref=ho.at[xc],
            dst_ref=ho.at[xc],
            send_sem=ho_ss.at[k],
            recv_sem=ho_rs.at[xc],
            device_id={"mp": z * 8 + (xc + k) % 8},
            device_id_type=MESH,
        )
        copy.start()
        ho_copies.append(copy)

    for k in range(1, 8):
        slot = (xc + k) % 8
        pltpu.make_async_remote_copy(
            src_ref=wo.at[slot],
            dst_ref=wo.at[slot],
            send_sem=w_ss.at[0],
            recv_sem=w_rs.at[slot],
            device_id={"mp": me},
            device_id_type=MESH,
        ).wait_recv()
    pltpu.make_async_copy(wo.at[xc], wo.at[xc], lsem.at[3]).wait()
    for k in range(1, 8):
        slot = (xc + k) % 8
        pltpu.make_async_remote_copy(
            src_ref=ho.at[slot],
            dst_ref=ho.at[slot],
            send_sem=ho_ss.at[0],
            recv_sem=ho_rs.at[slot],
            device_id={"mp": me},
            device_id_type=MESH,
        ).wait_recv()

    heads = jnp.concatenate([ho[j] for j in range(8)], axis=1)
    p_copies = []
    for k in (3, 2, 1, 0):
        zz = zo[k]
        right = jnp.concatenate([wo[j, zz] for j in range(8)], axis=0)
        part[zz] = dot(heads, right)
        if k > 0:
            copy = pltpu.make_async_remote_copy(
                src_ref=part.at[zz],
                dst_ref=rcv.at[z],
                send_sem=p_ss.at[k],
                recv_sem=p_rs.at[z],
                device_id={"mp": mp_of(zz, x, c)},
                device_id_type=MESH,
            )
            copy.start()
            p_copies.append(copy)
    result = part[z]
    for k in (1, 2, 3):
        zz = zo[k]
        pltpu.make_async_remote_copy(
            src_ref=rcv.at[zz],
            dst_ref=rcv.at[zz],
            send_sem=p_ss.at[0],
            recv_sem=p_rs.at[zz],
            device_id={"mp": me},
            device_id_type=MESH,
        ).wait_recv()
        result = result + rcv[zz]
    out[...] = result.astype(BF16)

    for copy in sends:
        copy.wait_send()
    for k in range(1, 8):
        pltpu.make_async_remote_copy(
            src_ref=wo.at[xc],
            dst_ref=wo.at[xc],
            send_sem=w_ss.at[k],
            recv_sem=w_rs.at[xc],
            device_id={"mp": me},
            device_id_type=MESH,
        ).wait_send()
    for copy in kv_copies + [doc_copy] + ho_copies + p_copies:
        copy.wait_send()


def shards(tokens, w_qkv, w_pos, w_out, content_bias, position_bias, doc_ids):
    vmem = pl.BlockSpec(memory_space=pltpu.VMEM)
    hbm = pl.BlockSpec(memory_space=pltpu.HBM)
    sinus = jnp.asarray(sinus_reversed(256, 4096))
    operands = (
        tokens, w_qkv, w_pos, w_out, content_bias, position_bias, doc_ids.reshape(1, 128), sinus
    )
    operands = [pltpu.with_memory_space_constraint(a, pltpu.HBM) for a in operands]
    return pl.pallas_call(
        kernel,
        out_shape=pltpu.VMEM((128, 128), BF16),
        in_specs=[hbm] * 8,
        out_specs=vmem,
        scratch_shapes=[
            pltpu.VMEM((1, 128), F32),
            pltpu.VMEM((1, 128), F32),
            pltpu.VMEM((1, 128), jnp.int32),
            pltpu.VMEM((32, 128, 128), BF16),
            pltpu.VMEM((3, 4096, 128), BF16),
            pltpu.VMEM((4096, 128), BF16),
            pltpu.VMEM((256, 4096), BF16),
            pltpu.VMEM((8, 4, 128, 128), BF16),
            pltpu.VMEM((128, 384), F32),
            pltpu.VMEM((2, 128, 128), BF16),
            pltpu.VMEM((2, 128, 128), BF16),
            pltpu.VMEM((1, 128), jnp.int32),
            pltpu.VMEM((8, 128, 128), BF16),
            pltpu.VMEM((4, 128, 128), F32),
            pltpu.VMEM((4, 128, 128), F32),
            pltpu.SemaphoreType.DMA((8,)),
            pltpu.SemaphoreType.DMA((31,)),
            pltpu.SemaphoreType.DMA((32,)),
            pltpu.SemaphoreType.DMA((8,)),
            pltpu.SemaphoreType.DMA((8,)),
            pltpu.SemaphoreType.DMA((3,)),
            pltpu.SemaphoreType.DMA((3,)),
            pltpu.SemaphoreType.DMA((8,)),
            pltpu.SemaphoreType.DMA((8,)),
            pltpu.SemaphoreType.DMA((4,)),
            pltpu.SemaphoreType.DMA((4,)),
        ],
        compiler_params=pltpu.CompilerParams(
            collective_id=0, has_side_effects=True, vmem_limit_bytes=20 * 1024 * 1024
        ),
        name="layer",
    )(*operands)


def solution(mesh):
    in_specs = (
        P("seq", "mp"),
        P(None, None, "mp"),
        P(None, "mp"),
        P("mp", None),
        P("mp", None),
        P("mp", None),
        P("seq"),
    )
    out_specs = P("seq", "mp")
    return jax.shard_map(shards, mesh=mesh, in_specs=in_specs, out_specs=out_specs, check_vma=False)
```

```python
import jax
import jax.numpy as jnp
import numpy as np
from jax import lax
from jax.experimental import pallas as pl
from jax.experimental.pallas import tpu as pltpu
from jax.sharding import PartitionSpec as P

MESH = pl.DeviceIdType.MESH
F32 = jnp.float32
BF16 = jnp.bfloat16


def sinus_reversed(count, width):
    place = np.arange(count, dtype=np.float32)[::-1, None]
    freqs = np.float32(1.0) / np.power(
        np.float32(10000.0), np.arange(0, width, 2, dtype=np.float32) / np.float32(width)
    )
    angle = place * freqs[None, :].astype(np.float32)
    table = np.concatenate([np.sin(angle), np.cos(angle)], axis=1)
    return table.astype(jnp.bfloat16)


def dot(a, b):
    return jnp.dot(a, b, preferred_element_type=F32)


def dot_t(a, b):
    return lax.dot_general(a, b, (((1,), (1,)), ((), ())), preferred_element_type=F32)


def kernel(
    tok_in, wqkv, wpos, wout, cbias_in, pbias_in, doc_in, sinus, out,
    cbias, pbias, doc, toks, wv, wp, sn, wo, acc, kvs, kvm, docm, ho, part, rcv,
    via, via_ss, via_rs, lsem, tok_ss, tok_rs, w_ss, w_rs, kv_ss, kv_rs, ho_ss, ho_rs, p_ss, p_rs,
):
    seq = lax.axis_index("seq")
    me = lax.axis_index("mp")
    n_seq = lax.axis_size("seq")
    z, x, c = me // 8, (me // 2) % 4, me % 2
    xc = me % 8
    nxt, prv = (seq + 1) % n_seq, (seq + n_seq - 1) % n_seq
    has_next, has_prev = seq < n_seq - 1, seq > 0
    xr, xl = (x + 1) % 4, (x + 3) % 4
    dirn = 1 - 2 * c
    x_up, x_dn = (x - dirn + 4) % 4, (x + dirn + 4) % 4
    x_far = (x + 2) % 4
    inner = (z // 2 + z % 2) % 2
    za, zb, zc = z + 1 - 2 * (z % 2), 3 - z, (z + 2) % 4
    zo = [z, za, inner * zb + (1 - inner) * zc, inner * zc + (1 - inner) * zb]

    def mp_of(zz, xx, cc):
        return (zz * 4 + xx) * 2 + cc

    barrier = pltpu.get_barrier_semaphore()
    for k in range(1, 8):
        pl.semaphore_signal(
            barrier, inc=1, device_id={"mp": z * 8 + (xc + k) % 8}, device_id_type=MESH
        )
    for k in range(1, 4):
        pl.semaphore_signal(
            barrier, inc=1, device_id={"mp": mp_of(zo[k], x, c)}, device_id_type=MESH
        )
    @pl.when(has_prev)
    def _():
        pl.semaphore_signal(barrier, inc=1, device_id={"seq": prv}, device_id_type=MESH)

    ld_tok = pltpu.make_async_copy(tok_in, toks.at[me], lsem.at[4])
    ld_tok.start()
    ld_doc = pltpu.make_async_copy(doc_in, doc, lsem.at[5])
    ld_doc.start()
    ld_cb = pltpu.make_async_copy(cbias_in, cbias, lsem.at[6])
    ld_cb.start()
    ld_pb = pltpu.make_async_copy(pbias_in, pbias, lsem.at[7])
    ld_pb.start()
    ld_sn = pltpu.make_async_copy(sinus, sn, lsem.at[0])
    ld_wp = pltpu.make_async_copy(wpos, wp, lsem.at[1])
    ld_wv = pltpu.make_async_copy(wqkv, wv, lsem.at[2])
    ld_sn.start()
    ld_wp.start()
    ld_wv.start()
    tok = toks.at[me]
    with jax.named_scope("m_tok"):
        ld_tok.wait()
        ld_doc.wait()

    with jax.named_scope("m_bar"):
        pl.semaphore_wait(barrier, 10 + has_next.astype(jnp.int32))

    sends = []

    def push(src, slot, target):
        n = len(sends)
        copy = pltpu.make_async_remote_copy(
            src_ref=src,
            dst_ref=toks.at[slot],
            send_sem=tok_ss.at[n],
            recv_sem=tok_rs.at[slot],
            device_id={"mp": target},
            device_id_type=MESH,
        )
        copy.start()
        sends.append(copy)

    def landed(slot):
        pltpu.make_async_remote_copy(
            src_ref=tok,
            dst_ref=toks.at[slot],
            send_sem=tok_ss.at[0],
            recv_sem=tok_rs.at[slot],
            device_id={"mp": me},
            device_id_type=MESH,
        ).wait_recv()

    push(tok, me, mp_of(zo[1], x, c))
    push(tok, me, mp_of(z, xr, c))
    push(tok, me, mp_of(z, xl, c))
    push(tok, me, mp_of(zo[2], x, c))
    push(tok, me, mp_of(zo[3], x, c))
    push(tok, me, mp_of(z, x, 1 - c))
    doc_copy = pltpu.make_async_remote_copy(
        src_ref=doc,
        dst_ref=docm,
        send_sem=kv_ss.at[2],
        recv_sem=kv_rs.at[2],
        device_id={"seq": nxt},
        device_id_type=MESH,
    )

    @pl.when(has_next)
    def _():
        doc_copy.start()

    with jax.named_scope("m_ldw"):
        ld_sn.wait()
        ld_wp.wait()
    with jax.named_scope("m_rel"):
        rel = dot(sn[...], wp[...]).astype(BF16)

    def blocks_of(to):
        for zz in range(4):
            yield zz, pl.ds(pl.multiple_of((zz * 8 + to) * 128, 128), 128)

    def share_weights():
        for n, (xx, cc) in enumerate(((xr, c), (xl, c), (xr, 1 - c), (xl, 1 - c), (x, 1 - c))):
            for zz, cols in blocks_of(xx * 2 + cc):
                pltpu.make_async_remote_copy(
                    src_ref=wout.at[:, cols],
                    dst_ref=wo.at[xc, zz],
                    send_sem=w_ss.at[n],
                    recv_sem=w_rs.at[xc],
                    device_id={"mp": mp_of(z, xx, cc)},
                    device_id_type=MESH,
                ).start()
        for n, cc in enumerate((0, 1)):
            for zz, cols in blocks_of(x_far * 2 + cc):
                pltpu.make_async_remote_copy(
                    src_ref=wout.at[:, cols],
                    dst_ref=via.at[n, zz],
                    send_sem=w_ss.at[5 + n],
                    recv_sem=via_rs.at[n],
                    device_id={"mp": mp_of(z, x_dn, c)},
                    device_id_type=MESH,
                ).start()
        for zz, cols in blocks_of(xc):
            pltpu.make_async_copy(wout.at[:, cols], wo.at[xc, zz], lsem.at[3]).start()

    def via_copy(n):
        slot = x_up * 2 + c
        return pltpu.make_async_remote_copy(
            src_ref=via.at[n],
            dst_ref=wo.at[slot],
            send_sem=via_ss.at[n],
            recv_sem=w_rs.at[slot],
            device_id={"mp": mp_of(z, x_dn, n)},
            device_id_type=MESH,
        )

    def relay_weights():
        for n in (0, 1):
            pltpu.make_async_remote_copy(
                src_ref=via.at[n],
                dst_ref=via.at[n],
                send_sem=via_ss.at[n],
                recv_sem=via_rs.at[n],
                device_id={"mp": me},
                device_id_type=MESH,
            ).wait_recv()
            via_copy(n).start()

    def from_z(k):
        slot = mp_of(zo[k], x, c)
        landed(slot)
        push(toks.at[slot], slot, mp_of(z, xr, c))
        push(toks.at[slot], slot, mp_of(z, xl, c))
        if k >= 2:
            push(toks.at[slot], slot, mp_of(z, x_far, c))
        push(toks.at[slot], slot, mp_of(z, x, 1 - c))

    def from_x(k):
        slot = mp_of(zo[k], x_up, c)
        landed(slot)
        if k < 2:
            push(toks.at[slot], slot, mp_of(z, x_dn, c))
        push(toks.at[slot], slot, mp_of(z, x, 1 - c))
        slot = mp_of(zo[k], x_dn, c)
        landed(slot)
        push(toks.at[slot], slot, mp_of(z, x, 1 - c))

    def from_far(k):
        slot = mp_of(zo[k], x_far, c)
        landed(slot)
        push(toks.at[slot], slot, mp_of(z, x, 1 - c))

    def from_core(k):
        for xx in (x, x_up, x_dn, x_far):
            landed(mp_of(zo[k], xx, 1 - c))

    def project(k):
        zz = zo[k]
        left = jnp.concatenate([toks[zz * 8 + j] for j in range(8)], axis=1)
        rows = pl.ds(pl.multiple_of(zz * 1024, 1024), 1024)
        right = jnp.concatenate([wv[0, rows, :], wv[1, rows, :], wv[2, rows, :]], axis=1)
        term = dot(left, right)
        if k == 0:
            acc[...] = term
        else:
            acc[...] += term

    for k in (1, 2, 3):
        with jax.named_scope(f"m_z{k}"):
            from_z(k)
    for k in (0, 1, 2, 3):
        with jax.named_scope(f"m_x{k}"):
            from_x(k)

    late = seq % 3 == 2

    @pl.when(jnp.logical_not(late))
    def _():
        share_weights()

    for k in (2, 3, 0, 1):
        with jax.named_scope(f"m_far{k}"):
            from_far(k)

    @pl.when(late)
    def _():
        share_weights()

    ld_wv.wait()
    for k in (0, 1, 2, 3):
        with jax.named_scope(f"m_core{k}"):
            from_core(k)
        with jax.named_scope(f"m_proj{k}"):
            project(k)

    kvs[0] = acc[:, 128:256].astype(BF16)
    kvs[1] = acc[:, 256:384].astype(BF16)
    kv_copies = []
    for i in range(2):
        copy = pltpu.make_async_remote_copy(
            src_ref=kvs.at[i],
            dst_ref=kvm.at[i],
            send_sem=kv_ss.at[i],
            recv_sem=kv_rs.at[i],
            device_id={"seq": nxt},
            device_id_type=MESH,
        )
        kv_copies.append(copy)

    @pl.when(has_next)
    def _():
        for copy in kv_copies:
            copy.start()

    ld_cb.wait()
    ld_pb.wait()
    query = acc[:, 0:128]
    qc = (query + cbias[...]).astype(BF16)
    qp = (query + pbias[...]).astype(BF16)
    pos = pltpu.roll(dot_t(qp, rel), 129, 1, stride=1, stride_axis=0)
    scale = F32(1.0) / jnp.sqrt(F32(128.0))
    own_doc = doc[...]
    row_doc = jnp.transpose(jnp.broadcast_to(own_doc, (128, 128)))
    rows = lax.broadcasted_iota(jnp.int32, (128, 128), 0)
    cols = lax.broadcasted_iota(jnp.int32, (128, 128), 1)
    ok_own = (cols <= rows) & (row_doc == own_doc)
    s_own = (dot_t(qc, kvs[0]) + pos[:, 128:256]) * scale
    s_own = jnp.where(ok_own, s_own, F32(-1e30))
    top_own = jnp.max(s_own, axis=1, keepdims=True)

    @pl.when(has_prev)
    def _():
        doc_copy.wait_recv()

    @pl.when(seq == 0)
    def _():
        docm[...] = jnp.zeros_like(docm)
        kvm[...] = jnp.zeros_like(kvm)

    ok_mem = (row_doc == docm[...]) & (seq > 0)
    for copy in sends:
        copy.wait_send()
    with jax.named_scope("m_via"):
        relay_weights()
    with jax.named_scope("m_kv0"):

        @pl.when(has_prev)
        def _():
            kv_copies[0].wait_recv()
    s_mem = (dot_t(qc, kvm[0]) + pos[:, 0:128]) * scale
    s_mem = jnp.where(ok_mem, s_mem, F32(-1e30))
    top = jnp.maximum(top_own, jnp.max(s_mem, axis=1, keepdims=True))
    e_own = jnp.where(ok_own, jnp.exp(s_own - top), F32(0.0))
    e_mem = jnp.where(ok_mem, jnp.exp(s_mem - top), F32(0.0))
    total = jnp.sum(e_own, axis=1, keepdims=True) + jnp.sum(e_mem, axis=1, keepdims=True)
    w_own = (e_own / total).astype(BF16)
    w_mem = (e_mem / total).astype(BF16)
    with jax.named_scope("m_kv1"):

        @pl.when(has_prev)
        def _():
            kv_copies[1].wait_recv()
    head = dot(w_own, kvs[1]) + dot(w_mem, kvm[1])
    ho[xc] = head.astype(BF16)

    ho_copies = []
    for k in (1, 7, 2, 6, 3, 5, 4):
        copy = pltpu.make_async_remote_copy(
            src_ref=ho.at[xc],
            dst_ref=ho.at[xc],
            send_sem=ho_ss.at[k],
            recv_sem=ho_rs.at[xc],
            device_id={"mp": z * 8 + (xc + k) % 8},
            device_id_type=MESH,
        )
        copy.start()
        ho_copies.append(copy)

    def weights_in(slot):
        pltpu.make_async_remote_copy(
            src_ref=wo.at[slot],
            dst_ref=wo.at[slot],
            send_sem=w_ss.at[0],
            recv_sem=w_rs.at[slot],
            device_id={"mp": me},
            device_id_type=MESH,
        ).wait_recv()

    def heads_in(slot):
        pltpu.make_async_remote_copy(
            src_ref=ho.at[slot],
            dst_ref=ho.at[slot],
            send_sem=ho_ss.at[0],
            recv_sem=ho_rs.at[slot],
            device_id={"mp": me},
            device_id_type=MESH,
        ).wait_recv()

    def pair_term(xs, zz):
        slots = [xx * 2 + cc for xx in xs for cc in (0, 1)]
        left = jnp.concatenate([ho[j] for j in slots], axis=1)
        right = jnp.concatenate([wo[j, zz] for j in slots], axis=0)
        return dot(left, right)

    with jax.named_scope("m_wo"):
        pltpu.make_async_copy(wo.at[xc], wo.at[xc], lsem.at[3]).wait()
        for slot in (x * 2 + 1 - c, xr * 2, xr * 2 + 1, xl * 2, xl * 2 + 1):
            weights_in(slot)
    with jax.named_scope("m_ho"):
        for slot in (x * 2 + 1 - c, xr * 2, xr * 2 + 1, xl * 2, xl * 2 + 1):
            heads_in(slot)
    for k in (3, 2, 1, 0):
        part[zo[k]] = pair_term((x, xr, xl), zo[k])
    with jax.named_scope("m_wof"):
        for slot in (x_far * 2, x_far * 2 + 1):
            weights_in(slot)
    with jax.named_scope("m_hof"):
        for slot in (x_far * 2, x_far * 2 + 1):
            heads_in(slot)
    p_copies = []
    for k in (3, 2, 1, 0):
        zz = zo[k]
        part[zz] += pair_term((x_far,), zz)
        if k > 0:
            copy = pltpu.make_async_remote_copy(
                src_ref=part.at[zz],
                dst_ref=rcv.at[z],
                send_sem=p_ss.at[k],
                recv_sem=p_rs.at[z],
                device_id={"mp": mp_of(zz, x, c)},
                device_id_type=MESH,
            )
            copy.start()
            p_copies.append(copy)

    for n in range(7):
        pltpu.make_async_remote_copy(
            src_ref=wo.at[xc],
            dst_ref=wo.at[xc],
            send_sem=w_ss.at[n],
            recv_sem=w_rs.at[xc],
            device_id={"mp": me},
            device_id_type=MESH,
        ).wait_send()
    for n in (0, 1):
        via_copy(n).wait_send()
    for copy in ho_copies:
        copy.wait_send()

    @pl.when(has_next)
    def _():
        for copy in kv_copies + [doc_copy]:
            copy.wait_send()

    result = part[z]
    for k in (1, 2, 3):
        zz = zo[k]
        with jax.named_scope(f"m_part{k}"):
            pltpu.make_async_remote_copy(
                src_ref=rcv.at[zz],
                dst_ref=rcv.at[zz],
                send_sem=p_ss.at[0],
                recv_sem=p_rs.at[zz],
                device_id={"mp": me},
                device_id_type=MESH,
            ).wait_recv()
        result = result + rcv[zz]
    out[...] = result.astype(BF16)

    with jax.named_scope("m_send"):
        for copy in p_copies:
            copy.wait_send()


def shards(tokens, w_qkv, w_pos, w_out, content_bias, position_bias, doc_ids):
    vmem = pl.BlockSpec(memory_space=pltpu.VMEM)
    hbm = pl.BlockSpec(memory_space=pltpu.HBM)
    sinus = jnp.asarray(sinus_reversed(256, 4096))
    operands = (
        tokens, w_qkv, w_pos, w_out, content_bias, position_bias, doc_ids.reshape(1, 128), sinus
    )
    operands = [pltpu.with_memory_space_constraint(a, pltpu.HBM) for a in operands]
    return pl.pallas_call(
        kernel,
        out_shape=pltpu.VMEM((128, 128), BF16),
        in_specs=[hbm] * 8,
        out_specs=vmem,
        scratch_shapes=[
            pltpu.VMEM((1, 128), F32),
            pltpu.VMEM((1, 128), F32),
            pltpu.VMEM((1, 128), jnp.int32),
            pltpu.VMEM((32, 128, 128), BF16),
            pltpu.VMEM((3, 4096, 128), BF16),
            pltpu.VMEM((4096, 128), BF16),
            pltpu.VMEM((256, 4096), BF16),
            pltpu.VMEM((8, 4, 128, 128), BF16),
            pltpu.VMEM((128, 384), F32),
            pltpu.VMEM((2, 128, 128), BF16),
            pltpu.VMEM((2, 128, 128), BF16),
            pltpu.VMEM((1, 128), jnp.int32),
            pltpu.VMEM((8, 128, 128), BF16),
            pltpu.VMEM((4, 128, 128), F32),
            pltpu.VMEM((4, 128, 128), F32),
            pltpu.VMEM((2, 4, 128, 128), BF16),
            pltpu.SemaphoreType.DMA((2,)),
            pltpu.SemaphoreType.DMA((2,)),
            pltpu.SemaphoreType.DMA((8,)),
            pltpu.SemaphoreType.DMA((31,)),
            pltpu.SemaphoreType.DMA((32,)),
            pltpu.SemaphoreType.DMA((8,)),
            pltpu.SemaphoreType.DMA((8,)),
            pltpu.SemaphoreType.DMA((3,)),
            pltpu.SemaphoreType.DMA((3,)),
            pltpu.SemaphoreType.DMA((8,)),
            pltpu.SemaphoreType.DMA((8,)),
            pltpu.SemaphoreType.DMA((4,)),
            pltpu.SemaphoreType.DMA((4,)),
        ],
        compiler_params=pltpu.CompilerParams(
            collective_id=0, has_side_effects=True, vmem_limit_bytes=20 * 1024 * 1024
        ),
        name="layer",
    )(*operands)


def solution(mesh):
    in_specs = (
        P("seq", "mp"),
        P(None, None, "mp"),
        P(None, "mp"),
        P("mp", None),
        P("mp", None),
        P("mp", None),
        P("seq"),
    )
    out_specs = P("seq", "mp")
    return jax.shard_map(shards, mesh=mesh, in_specs=in_specs, out_specs=out_specs, check_vma=False)
```

```python
import jax
import jax.numpy as jnp
import numpy as np
from jax import lax
from jax.experimental import pallas as pl
from jax.experimental.pallas import tpu as pltpu
from jax.sharding import PartitionSpec as P

MESH = pl.DeviceIdType.MESH
F32 = jnp.float32
BF16 = jnp.bfloat16
BANDS = 2


def sinus_reversed(count, width):
    place = np.arange(count, dtype=np.float32)[::-1, None]
    freqs = np.float32(1.0) / np.power(
        np.float32(10000.0), np.arange(0, width, 2, dtype=np.float32) / np.float32(width)
    )
    angle = place * freqs[None, :].astype(np.float32)
    table = np.concatenate([np.sin(angle), np.cos(angle)], axis=1)
    return table.astype(jnp.bfloat16)


def dot(a, b):
    return jnp.dot(a, b, preferred_element_type=F32)


def dot_t(a, b):
    return lax.dot_general(a, b, (((1,), (1,)), ((), ())), preferred_element_type=F32)


def kernel(
    tok_in, wqkv, wpos, wout, cbias_in, pbias_in, doc_in, sinus, out,
    cbias, pbias, doc, toks, wv, wp, sn, wo, acc, kvs, kvm, docm, ho, part, rcv,
    wst, via, ready, via_ss, via_rs, lsem, tok_ss, tok_rs, w_ss, w_rs, kv_ss, kv_rs, ho_ss, ho_rs, p_ss, p_rs,
):
    seq = lax.axis_index("seq")
    me = lax.axis_index("mp")
    n_seq = lax.axis_size("seq")
    z, x, c = me // 8, (me // 2) % 4, me % 2
    xc = me % 8
    nxt, prv = (seq + 1) % n_seq, (seq + n_seq - 1) % n_seq
    turn = seq % 3
    has_next, has_prev = seq < n_seq - 1, seq > 0
    xr, xl = (x + 1) % 4, (x + 3) % 4
    dirn = 1 - 2 * c
    x_up, x_dn = (x - dirn + 4) % 4, (x + dirn + 4) % 4
    x_far = (x + 2) % 4
    inner = (z // 2 + z % 2) % 2
    za, zb, zc = z + 1 - 2 * (z % 2), 3 - z, (z + 2) % 4
    zo = [z, za, inner * zb + (1 - inner) * zc, inner * zc + (1 - inner) * zb]

    peers = [(xr, c), (xl, c), (xr, 1 - c), (xl, 1 - c), (x, 1 - c), (x_far, c), (x_far, 1 - c)]

    def mp_of(zz, xx, cc):
        return (zz * 4 + xx) * 2 + cc

    barrier = pltpu.get_barrier_semaphore()
    for k in range(1, 8):
        pl.semaphore_signal(
            barrier, inc=1, device_id={"mp": z * 8 + (xc + k) % 8}, device_id_type=MESH
        )
    for k in range(1, 4):
        pl.semaphore_signal(
            barrier, inc=1, device_id={"mp": mp_of(zo[k], x, c)}, device_id_type=MESH
        )
    @pl.when(has_prev & (turn == 0))
    def _():
        pl.semaphore_signal(barrier, inc=1, device_id={"seq": prv}, device_id_type=MESH)

    @pl.when(turn != 2)
    def _():
        pl.semaphore_signal(barrier, inc=1, device_id={"seq": nxt}, device_id_type=MESH)

    ld_tok = pltpu.make_async_copy(tok_in, toks.at[me], lsem.at[4])
    ld_tok.start()
    ld_doc = pltpu.make_async_copy(doc_in, doc, lsem.at[5])
    ld_doc.start()
    ld_cb = pltpu.make_async_copy(cbias_in, cbias, lsem.at[6])
    ld_cb.start()
    ld_pb = pltpu.make_async_copy(pbias_in, pbias, lsem.at[7])
    ld_pb.start()
    ld_sn = pltpu.make_async_copy(sinus, sn, lsem.at[0])
    ld_wp = pltpu.make_async_copy(wpos, wp, lsem.at[1])
    ld_wv = pltpu.make_async_copy(wqkv, wv, lsem.at[2])
    ld_sn.start()
    ld_wp.start()
    ld_wv.start()
    for to in range(8):
        for zz in range(4):
            cols = pl.ds((zz * 8 + to) * 128, 128)
            pltpu.make_async_copy(wout.at[:, cols], wst.at[to, zz], lsem.at[8]).start()
    tok = toks.at[me]
    with jax.named_scope("m_tok"):
        ld_tok.wait()
        ld_doc.wait()

    with jax.named_scope("m_bar"):
        heard = (turn != 0).astype(jnp.int32) + (has_next & (turn == 2)).astype(jnp.int32)
        pl.semaphore_wait(barrier, 10 + heard)

    @pl.when(turn != 0)
    def _():
        pl.semaphore_signal(ready, inc=1, device_id={"seq": prv}, device_id_type=MESH)


    sends = []

    def push(src, slot, target):
        n = len(sends)
        copy = pltpu.make_async_remote_copy(
            src_ref=src,
            dst_ref=toks.at[slot],
            send_sem=tok_ss.at[n],
            recv_sem=tok_rs.at[slot],
            device_id={"mp": target},
            device_id_type=MESH,
        )
        copy.start()
        sends.append(copy)

    def landed(slot):
        pltpu.make_async_remote_copy(
            src_ref=tok,
            dst_ref=toks.at[slot],
            send_sem=tok_ss.at[0],
            recv_sem=tok_rs.at[slot],
            device_id={"mp": me},
            device_id_type=MESH,
        ).wait_recv()

    push(tok, me, mp_of(zo[1], x, c))
    push(tok, me, mp_of(z, xr, c))
    push(tok, me, mp_of(z, xl, c))
    push(tok, me, mp_of(z, x_far, c))
    push(tok, me, mp_of(zo[2], x, c))
    push(tok, me, mp_of(zo[3], x, c))
    push(tok, me, mp_of(z, x, 1 - c))
    doc_copy = pltpu.make_async_remote_copy(
        src_ref=doc,
        dst_ref=docm,
        send_sem=kv_ss.at[2],
        recv_sem=kv_rs.at[2],
        device_id={"seq": nxt},
        device_id_type=MESH,
    )

    @pl.when(has_next & (turn == 2))
    def _():
        doc_copy.start()

    with jax.named_scope("m_ldw"):
        ld_sn.wait()
        ld_wp.wait()
    with jax.named_scope("m_rel"):
        rel = dot(sn[...], wp[...]).astype(BF16)

    def share_weights():
        pltpu.make_async_copy(wst, wst, lsem.at[8]).wait()
        for n, cc in enumerate((0, 1)):
            pltpu.make_async_remote_copy(
                src_ref=wst.at[x_far * 2 + cc],
                dst_ref=via.at[n],
                send_sem=w_ss.at[5 + n],
                recv_sem=via_rs.at[n],
                device_id={"mp": mp_of(z, x_dn, c)},
                device_id_type=MESH,
            ).start()
        for n, (xx, cc) in enumerate(peers[:5]):
            pltpu.make_async_remote_copy(
                src_ref=wst.at[xx * 2 + cc],
                dst_ref=wo.at[xc],
                send_sem=w_ss.at[n],
                recv_sem=w_rs.at[xc],
                device_id={"mp": mp_of(z, xx, cc)},
                device_id_type=MESH,
            ).start()
        pltpu.make_async_copy(wst.at[xc], wo.at[xc], lsem.at[3]).start()

    def via_copy(n):
        slot = x_up * 2 + c
        return pltpu.make_async_remote_copy(
            src_ref=via.at[n],
            dst_ref=wo.at[slot],
            send_sem=via_ss.at[n],
            recv_sem=w_rs.at[slot],
            device_id={"mp": mp_of(z, x_dn, n)},
            device_id_type=MESH,
        )

    def relay_weights():
        for n in (0, 1):
            pltpu.make_async_remote_copy(
                src_ref=via.at[n],
                dst_ref=via.at[n],
                send_sem=via_ss.at[n],
                recv_sem=via_rs.at[n],
                device_id={"mp": me},
                device_id_type=MESH,
            ).wait_recv()
            via_copy(n).start()

    def from_z(k):
        slot = mp_of(zo[k], x, c)
        landed(slot)
        push(toks.at[slot], slot, mp_of(z, xr, c))
        push(toks.at[slot], slot, mp_of(z, xl, c))
        push(toks.at[slot], slot, mp_of(z, x, 1 - c))

    def from_x(k):
        slot = mp_of(zo[k], x_up, c)
        landed(slot)
        push(toks.at[slot], slot, mp_of(z, x, 1 - c))
        slot = mp_of(zo[k], x_dn, c)
        landed(slot)
        push(toks.at[slot], slot, mp_of(z, x, 1 - c))

    def from_far(k):
        slot = mp_of(zo[k], x_far, c)
        landed(slot)
        if k == 0:
            for j in (1, 2, 3):
                push(toks.at[slot], slot, mp_of(zo[j], x, c))
        push(toks.at[slot], slot, mp_of(z, x, 1 - c))

    def from_core(k):
        for xx in (x, x_up, x_dn, x_far):
            landed(mp_of(zo[k], xx, 1 - c))

    def project(k, cc):
        slots = [mp_of(zo[k], xx, cc) for xx in range(4)]
        left = jnp.concatenate([toks[j] for j in slots], axis=1)
        bands = [pl.ds(pl.multiple_of(j * 128, 128), 128) for j in slots]
        right = jnp.concatenate(
            [jnp.concatenate([wv[i, band, :] for band in bands], axis=0) for i in range(3)], axis=1
        )
        return dot(left, right)

    def at(name, step, k):
        with jax.named_scope(f"m_{name}{k}"):
            step(k)

    at("z", from_z, 1)
    at("z", from_z, 2)
    at("far", from_far, 0)
    at("z", from_z, 3)

    @pl.when(turn != 2)
    def _():
        share_weights()

    at("x", from_x, 0)
    for k in (1, 2, 3):
        at("x", from_x, k)
        at("far", from_far, k)

    @pl.when(turn == 2)
    def _():
        share_weights()

    ld_wv.wait()
    with jax.named_scope("m_same"):
        acc[...] = project(0, c)
        for k in (1, 2, 3):
            acc[...] += project(k, c)
    for k in (0, 1, 2, 3):
        at("core", from_core, k)
        acc[...] += project(k, 1 - c)

    kvs[0] = acc[:, 128:256].astype(BF16)
    kvs[1] = acc[:, 256:384].astype(BF16)
    kv_copies = []
    for i in range(2):
        copy = pltpu.make_async_remote_copy(
            src_ref=kvs.at[i],
            dst_ref=kvm.at[i],
            send_sem=kv_ss.at[i],
            recv_sem=kv_rs.at[i],
            device_id={"seq": nxt},
            device_id_type=MESH,
        )
        kv_copies.append(copy)

    @pl.when(turn != 2)
    def _():
        pl.semaphore_wait(ready, 1)

    @pl.when(turn != 2)
    def _():
        doc_copy.start()

    @pl.when(has_next & (turn != 1))
    def _():
        for copy in kv_copies:
            copy.start()

    ld_cb.wait()
    ld_pb.wait()
    query = acc[:, 0:128]
    qc = (query + cbias[...]).astype(BF16)
    qp = (query + pbias[...]).astype(BF16)
    pos = pltpu.roll(dot_t(qp, rel), 129, 1, stride=1, stride_axis=0)
    scale = F32(1.0) / jnp.sqrt(F32(128.0))
    own_doc = doc[...]
    row_doc = jnp.transpose(jnp.broadcast_to(own_doc, (128, 128)))
    rows = lax.broadcasted_iota(jnp.int32, (128, 128), 0)
    cols = lax.broadcasted_iota(jnp.int32, (128, 128), 1)
    ok_own = (cols <= rows) & (row_doc == own_doc)
    s_own = (dot_t(qc, kvs[0]) + pos[:, 128:256]) * scale
    s_own = jnp.where(ok_own, s_own, F32(-1e30))
    top_own = jnp.max(s_own, axis=1, keepdims=True)

    for copy in sends:
        copy.wait_send()
    with jax.named_scope("m_via"):
        relay_weights()

    @pl.when(has_prev)
    def _():
        doc_copy.wait_recv()

    @pl.when(seq == 0)
    def _():
        docm[...] = jnp.zeros_like(docm)
        kvm[...] = jnp.zeros_like(kvm)

    ok_mem = (row_doc == docm[...]) & (seq > 0)

    with jax.named_scope("m_kv0"):

        @pl.when(has_prev)
        def _():
            kv_copies[0].wait_recv()
    s_mem = (dot_t(qc, kvm[0]) + pos[:, 0:128]) * scale
    s_mem = jnp.where(ok_mem, s_mem, F32(-1e30))
    top = jnp.maximum(top_own, jnp.max(s_mem, axis=1, keepdims=True))
    e_own = jnp.where(ok_own, jnp.exp(s_own - top), F32(0.0))
    e_mem = jnp.where(ok_mem, jnp.exp(s_mem - top), F32(0.0))
    total = jnp.sum(e_own, axis=1, keepdims=True) + jnp.sum(e_mem, axis=1, keepdims=True)
    w_own = (e_own / total).astype(BF16)
    w_mem = (e_mem / total).astype(BF16)
    with jax.named_scope("m_kv1"):

        @pl.when(has_prev)
        def _():
            kv_copies[1].wait_recv()

    rows_in = 128 // BANDS
    ho_copies = []
    for half in range(BANDS):
        band = slice(half * rows_in, half * rows_in + rows_in)
        head = dot(w_own[band], kvs[1]) + dot(w_mem[band], kvm[1])
        ho[half, xc] = head.astype(BF16)
        for copy in ho_copies[-7:]:
            copy.wait_send()
        for n, (xx, cc) in enumerate(peers):
            copy = pltpu.make_async_remote_copy(
                src_ref=ho.at[half, xc],
                dst_ref=ho.at[half, xc],
                send_sem=ho_ss.at[half, n],
                recv_sem=ho_rs.at[half, xc],
                device_id={"mp": mp_of(z, xx, cc)},
                device_id_type=MESH,
            )
            copy.start()
            ho_copies.append(copy)

    def weights_in(slot):
        pltpu.make_async_remote_copy(
            src_ref=wo.at[slot],
            dst_ref=wo.at[slot],
            send_sem=w_ss.at[0],
            recv_sem=w_rs.at[slot],
            device_id={"mp": me},
            device_id_type=MESH,
        ).wait_recv()

    def heads_in(half, slot):
        pltpu.make_async_remote_copy(
            src_ref=ho.at[half, slot],
            dst_ref=ho.at[half, slot],
            send_sem=ho_ss.at[half, 0],
            recv_sem=ho_rs.at[half, slot],
            device_id={"mp": me},
            device_id_type=MESH,
        ).wait_recv()

    def term(half, xs, zz):
        slots = [xx * 2 + cc for xx in xs for cc in (0, 1)]
        left = jnp.concatenate([ho[half, j] for j in slots], axis=1)
        right = jnp.concatenate([wo[j, zz] for j in slots], axis=0)
        return dot(left, right)

    near = (x * 2 + 1 - c, xr * 2, xr * 2 + 1, xl * 2, xl * 2 + 1)
    far = (x_far * 2, x_far * 2 + 1)
    with jax.named_scope("m_wo"):
        pltpu.make_async_copy(wo.at[xc], wo.at[xc], lsem.at[3]).wait()
        for slot in near + far:
            weights_in(slot)

    @pl.when(turn == 1)
    def _():
        for copy in kv_copies:
            copy.start()

    p_copies = []
    for half in range(BANDS):
        with jax.named_scope(f"m_ho{half}"):
            for slot in near:
                heads_in(half, slot)
        for k in (3, 2, 1, 0):
            part[half, zo[k]] = term(half, (x, xr, xl), zo[k])
        with jax.named_scope(f"m_hof{half}"):
            for slot in far:
                heads_in(half, slot)
        for k in (3, 2, 1, 0):
            zz = zo[k]
            part[half, zz] += term(half, (x_far,), zz)
            if k > 0:
                copy = pltpu.make_async_remote_copy(
                    src_ref=part.at[half, zz],
                    dst_ref=rcv.at[half, z],
                    send_sem=p_ss.at[half, k],
                    recv_sem=p_rs.at[half, z],
                    device_id={"mp": mp_of(zz, x, c)},
                    device_id_type=MESH,
                )
                copy.start()
                p_copies.append(copy)

    for n in range(7):
        pltpu.make_async_remote_copy(
            src_ref=wo.at[xc],
            dst_ref=wo.at[xc],
            send_sem=w_ss.at[n],
            recv_sem=w_rs.at[xc],
            device_id={"mp": me},
            device_id_type=MESH,
        ).wait_send()
    for n in (0, 1):
        via_copy(n).wait_send()
    for copy in ho_copies[-7:]:
        copy.wait_send()

    @pl.when(has_next)
    def _():
        for copy in kv_copies + [doc_copy]:
            copy.wait_send()

    for half in range(BANDS):
        result = part[half, z]
        for k in (1, 2, 3):
            zz = zo[k]
            with jax.named_scope(f"m_part{half}{k}"):
                pltpu.make_async_remote_copy(
                    src_ref=rcv.at[half, zz],
                    dst_ref=rcv.at[half, zz],
                    send_sem=p_ss.at[half, 0],
                    recv_sem=p_rs.at[half, zz],
                    device_id={"mp": me},
                    device_id_type=MESH,
                ).wait_recv()
            result = result + rcv[half, zz]
        out[half * rows_in : half * rows_in + rows_in, :] = result.astype(BF16)

    with jax.named_scope("m_send"):
        for copy in p_copies:
            copy.wait_send()


def shards(tokens, w_qkv, w_pos, w_out, content_bias, position_bias, doc_ids):
    vmem = pl.BlockSpec(memory_space=pltpu.VMEM)
    hbm = pl.BlockSpec(memory_space=pltpu.HBM)
    sinus = jnp.asarray(sinus_reversed(256, 4096))
    operands = (
        tokens, w_qkv, w_pos, w_out, content_bias, position_bias, doc_ids.reshape(1, 128), sinus
    )
    operands = [pltpu.with_memory_space_constraint(a, pltpu.HBM) for a in operands]
    return pl.pallas_call(
        kernel,
        out_shape=pltpu.VMEM((128, 128), BF16),
        in_specs=[hbm] * 8,
        out_specs=vmem,
        scratch_shapes=[
            pltpu.VMEM((1, 128), F32),
            pltpu.VMEM((1, 128), F32),
            pltpu.VMEM((1, 128), jnp.int32),
            pltpu.VMEM((32, 128, 128), BF16),
            pltpu.VMEM((3, 4096, 128), BF16),
            pltpu.VMEM((4096, 128), BF16),
            pltpu.VMEM((256, 4096), BF16),
            pltpu.VMEM((8, 4, 128, 128), BF16),
            pltpu.VMEM((128, 384), F32),
            pltpu.VMEM((2, 128, 128), BF16),
            pltpu.VMEM((2, 128, 128), BF16),
            pltpu.VMEM((1, 128), jnp.int32),
            pltpu.VMEM((BANDS, 8, 128 // BANDS, 128), BF16),
            pltpu.VMEM((BANDS, 4, 128 // BANDS, 128), F32),
            pltpu.VMEM((BANDS, 4, 128 // BANDS, 128), F32),
            pltpu.VMEM((8, 4, 128, 128), BF16),
            pltpu.VMEM((2, 4, 128, 128), BF16),
            pltpu.SemaphoreType.REGULAR,
            pltpu.SemaphoreType.DMA((2,)),
            pltpu.SemaphoreType.DMA((2,)),
            pltpu.SemaphoreType.DMA((9,)),
            pltpu.SemaphoreType.DMA((31,)),
            pltpu.SemaphoreType.DMA((32,)),
            pltpu.SemaphoreType.DMA((8,)),
            pltpu.SemaphoreType.DMA((8,)),
            pltpu.SemaphoreType.DMA((3,)),
            pltpu.SemaphoreType.DMA((3,)),
            pltpu.SemaphoreType.DMA((BANDS, 7)),
            pltpu.SemaphoreType.DMA((BANDS, 8)),
            pltpu.SemaphoreType.DMA((BANDS, 4)),
            pltpu.SemaphoreType.DMA((BANDS, 4)),
        ],
        compiler_params=pltpu.CompilerParams(
            collective_id=0, has_side_effects=True, vmem_limit_bytes=20 * 1024 * 1024
        ),
        name="layer",
    )(*operands)


def solution(mesh):
    in_specs = (
        P("seq", "mp"),
        P(None, None, "mp"),
        P(None, "mp"),
        P("mp", None),
        P("mp", None),
        P("mp", None),
        P("seq"),
    )
    out_specs = P("seq", "mp")
    return jax.shard_map(shards, mesh=mesh, in_specs=in_specs, out_specs=out_specs, check_vma=False)
```

```python
import jax
import jax.numpy as jnp
import numpy as np
from jax import lax
from jax.experimental import pallas as pl
from jax.experimental.pallas import tpu as pltpu
from jax.sharding import PartitionSpec as P

MESH = pl.DeviceIdType.MESH
F32 = jnp.float32
BF16 = jnp.bfloat16
BANDS = 2


def sinus_reversed(count, width):
    place = np.arange(count, dtype=np.float32)[::-1, None]
    freqs = np.float32(1.0) / np.power(
        np.float32(10000.0), np.arange(0, width, 2, dtype=np.float32) / np.float32(width)
    )
    angle = place * freqs[None, :].astype(np.float32)
    table = np.concatenate([np.sin(angle), np.cos(angle)], axis=1)
    return table.astype(jnp.bfloat16)


def dot(a, b):
    return jnp.dot(a, b, preferred_element_type=F32)


def dot_t(a, b):
    return lax.dot_general(a, b, (((1,), (1,)), ((), ())), preferred_element_type=F32)


def kernel(
    tok_in, wqkv, wpos, wout, cbias_in, pbias_in, doc_in, sinus, out,
    cbias, pbias, doc, toks, wv, wp, sn, wo, acc, kvs, kvm, docm, ho, part, rcv,
    wst, via, ready, via_ss, via_rs, lsem, tok_ss, tok_rs, core_rs, w_ss, w_rs, kv_ss, kv_rs, ho_ss, ho_rs, p_ss, p_rs,
):
    seq = lax.axis_index("seq")
    me = lax.axis_index("mp")
    n_seq = lax.axis_size("seq")
    z, x, c = me // 8, (me // 2) % 4, me % 2
    xc = me % 8
    nxt, prv = (seq + 1) % n_seq, (seq + n_seq - 1) % n_seq
    turn = seq % 3
    has_next, has_prev = seq < n_seq - 1, seq > 0
    xr, xl = (x + 1) % 4, (x + 3) % 4
    dirn = 1 - 2 * c
    x_up, x_dn = (x - dirn + 4) % 4, (x + dirn + 4) % 4
    x_far = (x + 2) % 4
    inner = (z // 2 + z % 2) % 2
    za, zb, zc = z + 1 - 2 * (z % 2), 3 - z, (z + 2) % 4
    zo = [z, za, inner * zb + (1 - inner) * zc, inner * zc + (1 - inner) * zb]

    peers = [(xr, c), (xl, c), (xr, 1 - c), (xl, 1 - c), (x, 1 - c), (x_far, c), (x_far, 1 - c)]

    def mp_of(zz, xx, cc):
        return (zz * 4 + xx) * 2 + cc

    barrier = pltpu.get_barrier_semaphore()
    for k in range(1, 8):
        pl.semaphore_signal(
            barrier, inc=1, device_id={"mp": z * 8 + (xc + k) % 8}, device_id_type=MESH
        )
    for k in range(1, 4):
        pl.semaphore_signal(
            barrier, inc=1, device_id={"mp": mp_of(zo[k], x, c)}, device_id_type=MESH
        )
    @pl.when(has_prev & (turn == 0))
    def _():
        pl.semaphore_signal(barrier, inc=1, device_id={"seq": prv}, device_id_type=MESH)

    @pl.when(turn != 2)
    def _():
        pl.semaphore_signal(barrier, inc=1, device_id={"seq": nxt}, device_id_type=MESH)

    ld_tok = [
        pltpu.make_async_copy(tok_in.at[pl.ds(h * 64, 64)], toks.at[h, me], lsem.at[9 + h])
        for h in (0, 1)
    ]
    for copy in ld_tok:
        copy.start()
    ld_doc = pltpu.make_async_copy(doc_in, doc, lsem.at[5])
    ld_doc.start()
    ld_cb = pltpu.make_async_copy(cbias_in, cbias, lsem.at[6])
    ld_cb.start()
    ld_pb = pltpu.make_async_copy(pbias_in, pbias, lsem.at[7])
    ld_pb.start()
    ld_sn = pltpu.make_async_copy(sinus, sn, lsem.at[0])
    ld_wp = pltpu.make_async_copy(wpos, wp, lsem.at[1])
    ld_wv = pltpu.make_async_copy(wqkv, wv, lsem.at[2])
    ld_sn.start()
    ld_wp.start()
    ld_wv.start()
    with jax.named_scope("m_tok"):
        for copy in ld_tok:
            copy.wait()
        ld_doc.wait()

    with jax.named_scope("m_bar"):
        heard = (turn != 0).astype(jnp.int32) + (has_next & (turn == 2)).astype(jnp.int32)
        pl.semaphore_wait(barrier, 10 + heard)

    @pl.when(turn != 0)
    def _():
        pl.semaphore_signal(ready, inc=1, device_id={"seq": prv}, device_id_type=MESH)


    sends = [0, 0]

    def sent(all_of, sem):
        pltpu.make_async_remote_copy(
            src_ref=all_of,
            dst_ref=all_of,
            send_sem=sem,
            recv_sem=via_rs.at[0],
            device_id={"mp": me},
            device_id_type=MESH,
        ).wait_send()

    def arrived(all_of, sem):
        pltpu.make_async_remote_copy(
            src_ref=all_of,
            dst_ref=all_of,
            send_sem=via_ss,
            recv_sem=sem,
            device_id={"mp": me},
            device_id_type=MESH,
        ).wait_recv()

    def push(h, slot, target, partner=False):
        copy = pltpu.make_async_remote_copy(
            src_ref=toks.at[h, slot],
            dst_ref=toks.at[h, slot],
            send_sem=tok_ss.at[h],
            recv_sem=core_rs.at[h, slot // 8] if partner else tok_rs.at[h, slot // 2],
            device_id={"mp": target},
            device_id_type=MESH,
        )
        copy.start()
        sends[h] += 1

    def landed(h, slot):
        pltpu.make_async_remote_copy(
            src_ref=toks.at[h, slot],
            dst_ref=toks.at[h, slot],
            send_sem=tok_ss.at[h],
            recv_sem=tok_rs.at[h, slot // 2],
            device_id={"mp": me},
            device_id_type=MESH,
        ).wait_recv()

    def own(h):
        push(h, me, mp_of(zo[1], x, c))
        push(h, me, mp_of(z, xr, c))
        push(h, me, mp_of(z, xl, c))
        push(h, me, mp_of(z, x_far, c))
        push(h, me, mp_of(zo[2], x, c))
        push(h, me, mp_of(zo[3], x, c))
        push(h, me, mp_of(z, x, 1 - c), True)

    own(0)
    for to in range(8):
        for zz in range(4):
            cols = pl.ds((zz * 8 + to) * 128, 128)
            pltpu.make_async_copy(wout.at[:, cols], wst.at[to, zz], lsem.at[8]).start()
    doc_copy = pltpu.make_async_remote_copy(
        src_ref=doc,
        dst_ref=docm,
        send_sem=kv_ss.at[4],
        recv_sem=kv_rs.at[4],
        device_id={"seq": nxt},
        device_id_type=MESH,
    )

    @pl.when(has_next & (turn == 2))
    def _():
        doc_copy.start()

    with jax.named_scope("m_ldw"):
        ld_sn.wait()
        ld_wp.wait()
    with jax.named_scope("m_rel"):
        rel = dot(sn[...], wp[...]).astype(BF16)
    own(1)

    def share_weights():
        pltpu.make_async_copy(wst, wst, lsem.at[8]).wait()
        for n, cc in enumerate((0, 1)):
            pltpu.make_async_remote_copy(
                src_ref=wst.at[x_far * 2 + cc],
                dst_ref=via.at[n],
                send_sem=w_ss,
                recv_sem=via_rs.at[n],
                device_id={"mp": mp_of(z, x_dn, c)},
                device_id_type=MESH,
            ).start()
        for n, (xx, cc) in enumerate(peers[:5]):
            pltpu.make_async_remote_copy(
                src_ref=wst.at[xx * 2 + cc],
                dst_ref=wo.at[xc],
                send_sem=w_ss,
                recv_sem=w_rs,
                device_id={"mp": mp_of(z, xx, cc)},
                device_id_type=MESH,
            ).start()
        pltpu.make_async_copy(wst.at[xc], wo.at[xc], lsem.at[3]).start()

    def via_copy(n):
        slot = x_up * 2 + c
        return pltpu.make_async_remote_copy(
            src_ref=via.at[n],
            dst_ref=wo.at[slot],
            send_sem=via_ss,
            recv_sem=w_rs,
            device_id={"mp": mp_of(z, x_dn, n)},
            device_id_type=MESH,
        )

    def relay_weights():
        for n in (0, 1):
            arrived(via.at[n], via_rs.at[n])
            via_copy(n).start()

    def from_z(h, k):
        slot = mp_of(zo[k], x, c)
        landed(h, slot)
        push(h, slot, mp_of(z, xr, c))
        push(h, slot, mp_of(z, xl, c))
        push(h, slot, mp_of(z, x, 1 - c), True)

    def from_x(h, k):
        for xx in (x_up, x_dn):
            slot = mp_of(zo[k], xx, c)
            landed(h, slot)
            push(h, slot, mp_of(z, x, 1 - c), True)

    def from_far(h, k):
        slot = mp_of(zo[k], x_far, c)
        landed(h, slot)
        if k == 0:
            for j in (1, 2, 3):
                push(h, slot, mp_of(zo[j], x, c))
        push(h, slot, mp_of(z, x, 1 - c), True)

    def from_core(h, k):
        four = toks.at[h, pl.ds(0, 4)]
        pltpu.make_async_remote_copy(
            src_ref=four,
            dst_ref=four,
            send_sem=tok_ss.at[h],
            recv_sem=core_rs.at[h, zo[k]],
            device_id={"mp": me},
            device_id_type=MESH,
        ).wait_recv()

    def project(h, k, cc):
        slots = [mp_of(zo[k], xx, cc) for xx in range(4)]
        left = jnp.concatenate([toks[h, j] for j in slots], axis=1)
        bands = [pl.ds(pl.multiple_of(j * 128, 128), 128) for j in slots]
        right = jnp.concatenate(
            [jnp.concatenate([wv[i, band, :] for band in bands], axis=0) for i in range(3)], axis=1
        )
        return dot(left, right)

    def at(name, step, h, k):
        with jax.named_scope(f"m_{name}{h}{k}"):
            step(h, k)

    def across(h):
        at("z", from_z, h, 1)
        at("z", from_z, h, 2)
        at("far", from_far, h, 0)
        at("z", from_z, h, 3)

    def along(h, ks):
        for k in ks:
            at("x", from_x, h, k)
            if k > 0:
                at("far", from_far, h, k)

    def same(h):
        half = slice(h * 64, h * 64 + 64)
        with jax.named_scope(f"m_same{h}"):
            acc[half] = project(h, 0, c)
            for k in (1, 2, 3):
                acc[half] += project(h, k, c)

    def other(h):
        half = slice(h * 64, h * 64 + 64)
        for k in (0, 1, 2, 3):
            at("core", from_core, h, k)
            acc[half] += project(h, k, 1 - c)
        kvs[0, half] = acc[half, 128:256].astype(BF16)
        kvs[1, half] = acc[half, 256:384].astype(BF16)

    kv_copies = []
    for h in (0, 1):
        for i in (0, 1):
            kv_copies.append(
                pltpu.make_async_remote_copy(
                    src_ref=kvs.at[i, pl.ds(h * 64, 64)],
                    dst_ref=kvm.at[i, pl.ds(h * 64, 64)],
                    send_sem=kv_ss.at[h * 2 + i],
                    recv_sem=kv_rs.at[h * 2 + i],
                    device_id={"seq": nxt},
                    device_id_type=MESH,
                )
            )

    def pass_on(h):
        @pl.when(has_next & (turn != 1))
        def _():
            for copy in kv_copies[2 * h : 2 * h + 2]:
                copy.start()

    across(0)
    across(1)

    @pl.when(turn != 2)
    def _():
        share_weights()

    along(0, (0, 1, 2, 3))
    ld_wv.wait()
    same(0)
    along(1, (0, 1))
    other(0)

    @pl.when(turn != 2)
    def _():
        pl.semaphore_wait(ready, 1)
        doc_copy.start()

    pass_on(0)
    along(1, (2, 3))

    @pl.when(turn == 2)
    def _():
        share_weights()

    same(1)
    other(1)
    pass_on(1)

    ld_cb.wait()
    ld_pb.wait()
    query = acc[:, 0:128]
    qc = (query + cbias[...]).astype(BF16)
    qp = (query + pbias[...]).astype(BF16)
    pos = pltpu.roll(dot_t(qp, rel), 129, 1, stride=1, stride_axis=0)
    scale = F32(1.0) / jnp.sqrt(F32(128.0))
    own_doc = doc[...]
    row_doc = jnp.transpose(jnp.broadcast_to(own_doc, (128, 128)))
    rows = lax.broadcasted_iota(jnp.int32, (128, 128), 0)
    cols = lax.broadcasted_iota(jnp.int32, (128, 128), 1)
    ok_own = (cols <= rows) & (row_doc == own_doc)
    s_own = (dot_t(qc, kvs[0]) + pos[:, 128:256]) * scale
    s_own = jnp.where(ok_own, s_own, F32(-1e30))
    top_own = jnp.max(s_own, axis=1, keepdims=True)

    for h in (0, 1):
        sent(toks.at[h, pl.ds(0, sends[h])], tok_ss.at[h])
    with jax.named_scope("m_via"):
        relay_weights()

    @pl.when(has_prev)
    def _():
        doc_copy.wait_recv()

    @pl.when(seq == 0)
    def _():
        docm[...] = jnp.zeros_like(docm)
        kvm[...] = jnp.zeros_like(kvm)

    ok_mem = (row_doc == docm[...]) & (seq > 0)

    with jax.named_scope("m_kv0"):

        @pl.when(has_prev)
        def _():
            for copy in kv_copies[0:3]:
                copy.wait_recv()
    s_mem = (dot_t(qc, kvm[0]) + pos[:, 0:128]) * scale
    s_mem = jnp.where(ok_mem, s_mem, F32(-1e30))
    top = jnp.maximum(top_own, jnp.max(s_mem, axis=1, keepdims=True))
    e_own = jnp.where(ok_own, jnp.exp(s_own - top), F32(0.0))
    e_mem = jnp.where(ok_mem, jnp.exp(s_mem - top), F32(0.0))
    total = jnp.sum(e_own, axis=1, keepdims=True) + jnp.sum(e_mem, axis=1, keepdims=True)
    w_own = (e_own / total).astype(BF16)
    w_mem = (e_mem / total).astype(BF16)
    with jax.named_scope("m_kv1"):

        @pl.when(has_prev)
        def _():
            kv_copies[3].wait_recv()

    rows_in = 128 // BANDS
    for half in range(BANDS):
        band = slice(half * rows_in, half * rows_in + rows_in)
        head = dot(w_own[band], kvs[1]) + dot(w_mem[band], kvm[1])
        ho[half, xc] = head.astype(BF16)
        if half > 0:
            sent(ho.at[half - 1, pl.ds(0, 7)], ho_ss.at[half - 1])
        for n, (xx, cc) in enumerate(peers):
            copy = pltpu.make_async_remote_copy(
                src_ref=ho.at[half, xc],
                dst_ref=ho.at[half, xc],
                send_sem=ho_ss.at[half],
                recv_sem=ho_rs.at[half, n // 5],
                device_id={"mp": mp_of(z, xx, cc)},
                device_id_type=MESH,
            )
            copy.start()

    def term(half, xs, zz):
        slots = [xx * 2 + cc for xx in xs for cc in (0, 1)]
        left = jnp.concatenate([ho[half, j] for j in slots], axis=1)
        right = jnp.concatenate([wo[j, zz] for j in slots], axis=0)
        return dot(left, right)

    with jax.named_scope("m_wo"):
        pltpu.make_async_copy(wo.at[xc], wo.at[xc], lsem.at[3]).wait()
        arrived(wo.at[pl.ds(0, 7)], w_rs)

    @pl.when(turn == 1)
    def _():
        for copy in kv_copies:
            copy.start()

    for half in range(BANDS):
        with jax.named_scope(f"m_ho{half}"):
            arrived(ho.at[half, pl.ds(0, 5)], ho_rs.at[half, 0])
        for k in (3, 2, 1, 0):
            part[half, zo[k]] = term(half, (x, xr, xl), zo[k])
        with jax.named_scope(f"m_hof{half}"):
            arrived(ho.at[half, pl.ds(0, 2)], ho_rs.at[half, 1])
        for k in (3, 2, 1, 0):
            zz = zo[k]
            part[half, zz] += term(half, (x_far,), zz)
            if k > 0:
                copy = pltpu.make_async_remote_copy(
                    src_ref=part.at[half, zz],
                    dst_ref=rcv.at[half, z],
                    send_sem=p_ss.at[half],
                    recv_sem=p_rs.at[half],
                    device_id={"mp": mp_of(zz, x, c)},
                    device_id_type=MESH,
                )
                copy.start()

    sent(wst.at[pl.ds(0, 7)], w_ss)
    sent(via, via_ss)
    sent(ho.at[BANDS - 1, pl.ds(0, 7)], ho_ss.at[BANDS - 1])

    @pl.when(has_next)
    def _():
        for copy in kv_copies + [doc_copy]:
            copy.wait_send()

    for half in range(BANDS):
        with jax.named_scope(f"m_part{half}"):
            arrived(rcv.at[half, pl.ds(0, 3)], p_rs.at[half])
        result = part[half, z]
        for k in (1, 2, 3):
            result = result + rcv[half, zo[k]]
        out[half * rows_in : half * rows_in + rows_in, :] = result.astype(BF16)

    with jax.named_scope("m_send"):
        for half in range(BANDS):
            sent(part.at[half, pl.ds(0, 3)], p_ss.at[half])


def shards(tokens, w_qkv, w_pos, w_out, content_bias, position_bias, doc_ids):
    vmem = pl.BlockSpec(memory_space=pltpu.VMEM)
    hbm = pl.BlockSpec(memory_space=pltpu.HBM)
    sinus = jnp.asarray(sinus_reversed(256, 4096))
    operands = (
        tokens, w_qkv, w_pos, w_out, content_bias, position_bias, doc_ids.reshape(1, 128), sinus
    )
    operands = [pltpu.with_memory_space_constraint(a, pltpu.HBM) for a in operands]
    return pl.pallas_call(
        kernel,
        out_shape=pltpu.VMEM((128, 128), BF16),
        in_specs=[hbm] * 8,
        out_specs=vmem,
        scratch_shapes=[
            pltpu.VMEM((1, 128), F32),
            pltpu.VMEM((1, 128), F32),
            pltpu.VMEM((1, 128), jnp.int32),
            pltpu.VMEM((2, 32, 64, 128), BF16),
            pltpu.VMEM((3, 4096, 128), BF16),
            pltpu.VMEM((4096, 128), BF16),
            pltpu.VMEM((256, 4096), BF16),
            pltpu.VMEM((8, 4, 128, 128), BF16),
            pltpu.VMEM((128, 384), F32),
            pltpu.VMEM((2, 128, 128), BF16),
            pltpu.VMEM((2, 128, 128), BF16),
            pltpu.VMEM((1, 128), jnp.int32),
            pltpu.VMEM((BANDS, 8, 128 // BANDS, 128), BF16),
            pltpu.VMEM((BANDS, 4, 128 // BANDS, 128), F32),
            pltpu.VMEM((BANDS, 4, 128 // BANDS, 128), F32),
            pltpu.VMEM((8, 4, 128, 128), BF16),
            pltpu.VMEM((2, 4, 128, 128), BF16),
            pltpu.SemaphoreType.REGULAR,
            pltpu.SemaphoreType.DMA,
            pltpu.SemaphoreType.DMA((2,)),
            pltpu.SemaphoreType.DMA((11,)),
            pltpu.SemaphoreType.DMA((2,)),
            pltpu.SemaphoreType.DMA((2, 16)),
            pltpu.SemaphoreType.DMA((2, 4)),
            pltpu.SemaphoreType.DMA,
            pltpu.SemaphoreType.DMA,
            pltpu.SemaphoreType.DMA((5,)),
            pltpu.SemaphoreType.DMA((5,)),
            pltpu.SemaphoreType.DMA((BANDS,)),
            pltpu.SemaphoreType.DMA((BANDS, 2)),
            pltpu.SemaphoreType.DMA((BANDS,)),
            pltpu.SemaphoreType.DMA((BANDS,)),
        ],
        compiler_params=pltpu.CompilerParams(
            collective_id=0, has_side_effects=True, vmem_limit_bytes=20 * 1024 * 1024
        ),
        name="layer",
    )(*operands)


def solution(mesh):
    in_specs = (
        P("seq", "mp"),
        P(None, None, "mp"),
        P(None, "mp"),
        P("mp", None),
        P("mp", None),
        P("mp", None),
        P("seq"),
    )
    out_specs = P("seq", "mp")
    return jax.shard_map(shards, mesh=mesh, in_specs=in_specs, out_specs=out_specs, check_vma=False)
```

```python
import jax
import jax.numpy as jnp
import numpy as np
from jax import lax
from jax.experimental import pallas as pl
from jax.experimental.pallas import tpu as pltpu
from jax.sharding import PartitionSpec as P

MESH = pl.DeviceIdType.MESH
F32 = jnp.float32
BF16 = jnp.bfloat16
BANDS = 2


def sinus_reversed(count, width):
    place = np.arange(count, dtype=np.float32)[::-1, None]
    freqs = np.float32(1.0) / np.power(
        np.float32(10000.0), np.arange(0, width, 2, dtype=np.float32) / np.float32(width)
    )
    angle = place * freqs[None, :].astype(np.float32)
    table = np.concatenate([np.sin(angle), np.cos(angle)], axis=1)
    return table.astype(jnp.bfloat16)


def dot(a, b):
    return jnp.dot(a, b, preferred_element_type=F32)


def dot_t(a, b):
    return lax.dot_general(a, b, (((1,), (1,)), ((), ())), preferred_element_type=F32)


def kernel(
    tok_in, wqkv, wpos, wout, cbias_in, pbias_in, doc_in, sinus, out,
    cbias, pbias, doc, toks, wv, wp, sn, wo, acc, kvs, kvm, docm, ho, part, rcv,
    wst, via, ready, via_ss, via_rs, lsem, tok_ss, tok_rs, core_rs, w_ss, w_rs, kv_ss, kv_rs, ho_ss, ho_rs, p_ss, p_rs,
):
    seq = lax.axis_index("seq")
    me = lax.axis_index("mp")
    n_seq = lax.axis_size("seq")
    z, x, c = me // 8, (me // 2) % 4, me % 2
    xc = me % 8
    nxt, prv = (seq + 1) % n_seq, (seq + n_seq - 1) % n_seq
    turn = seq % 3
    has_next, has_prev = seq < n_seq - 1, seq > 0
    xr, xl = (x + 1) % 4, (x + 3) % 4
    dirn = 1 - 2 * c
    x_up, x_dn = (x - dirn + 4) % 4, (x + dirn + 4) % 4
    x_far = (x + 2) % 4
    inner = (z // 2 + z % 2) % 2
    za, zb, zc = z + 1 - 2 * (z % 2), 3 - z, (z + 2) % 4
    zo = [z, za, inner * zb + (1 - inner) * zc, inner * zc + (1 - inner) * zb]

    peers = [(xr, c), (xl, c), (xr, 1 - c), (xl, 1 - c), (x, 1 - c), (x_far, c), (x_far, 1 - c)]

    def mp_of(zz, xx, cc):
        return (zz * 4 + xx) * 2 + cc

    barrier = pltpu.get_barrier_semaphore()
    for k in range(1, 8):
        pl.semaphore_signal(
            barrier, inc=1, device_id={"mp": z * 8 + (xc + k) % 8}, device_id_type=MESH
        )
    for k in range(1, 4):
        pl.semaphore_signal(
            barrier, inc=1, device_id={"mp": mp_of(zo[k], x, c)}, device_id_type=MESH
        )
    @pl.when(has_prev & (turn == 0))
    def _():
        pl.semaphore_signal(barrier, inc=1, device_id={"seq": prv}, device_id_type=MESH)

    @pl.when(turn != 2)
    def _():
        pl.semaphore_signal(barrier, inc=1, device_id={"seq": nxt}, device_id_type=MESH)

    ld_tok = [
        pltpu.make_async_copy(tok_in.at[pl.ds(h * 64, 64)], toks.at[h, me], lsem.at[9 + h])
        for h in (0, 1)
    ]
    for copy in ld_tok:
        copy.start()
    ld_doc = pltpu.make_async_copy(doc_in, doc, lsem.at[5])
    ld_doc.start()
    ld_cb = pltpu.make_async_copy(cbias_in, cbias, lsem.at[6])
    ld_cb.start()
    ld_pb = pltpu.make_async_copy(pbias_in, pbias, lsem.at[7])
    ld_pb.start()
    ld_sn = pltpu.make_async_copy(sinus, sn, lsem.at[0])
    ld_wp = pltpu.make_async_copy(wpos, wp, lsem.at[1])
    ld_wv = pltpu.make_async_copy(wqkv, wv, lsem.at[2])
    ld_sn.start()
    ld_wp.start()
    ld_wv.start()
    with jax.named_scope("m_tok"):
        for copy in ld_tok:
            copy.wait()
        ld_doc.wait()

    with jax.named_scope("m_bar"):
        heard = (turn != 0).astype(jnp.int32) + (has_next & (turn == 2)).astype(jnp.int32)
        pl.semaphore_wait(barrier, 10 + heard)

    @pl.when(turn != 0)
    def _():
        pl.semaphore_signal(ready, inc=1, device_id={"seq": prv}, device_id_type=MESH)


    sends = [0, 0]

    def sent(all_of, sem):
        pltpu.make_async_remote_copy(
            src_ref=all_of,
            dst_ref=all_of,
            send_sem=sem,
            recv_sem=via_rs.at[0],
            device_id={"mp": me},
            device_id_type=MESH,
        ).wait_send()

    def arrived(all_of, sem):
        pltpu.make_async_remote_copy(
            src_ref=all_of,
            dst_ref=all_of,
            send_sem=via_ss,
            recv_sem=sem,
            device_id={"mp": me},
            device_id_type=MESH,
        ).wait_recv()

    def push(h, slot, target, partner=False):
        copy = pltpu.make_async_remote_copy(
            src_ref=toks.at[h, slot],
            dst_ref=toks.at[h, slot],
            send_sem=tok_ss.at[h],
            recv_sem=core_rs.at[h, slot // 8] if partner else tok_rs.at[h, slot // 2],
            device_id={"mp": target},
            device_id_type=MESH,
        )
        copy.start()
        sends[h] += 1

    def landed(h, slot):
        pltpu.make_async_remote_copy(
            src_ref=toks.at[h, slot],
            dst_ref=toks.at[h, slot],
            send_sem=tok_ss.at[h],
            recv_sem=tok_rs.at[h, slot // 2],
            device_id={"mp": me},
            device_id_type=MESH,
        ).wait_recv()

    def own(h):
        push(h, me, mp_of(zo[1], x, c))
        push(h, me, mp_of(z, xr, c))
        push(h, me, mp_of(z, xl, c))
        push(h, me, mp_of(z, x_far, c))
        push(h, me, mp_of(zo[2], x, c))
        push(h, me, mp_of(zo[3], x, c))
        push(h, me, mp_of(z, x, 1 - c), True)

    own(0)
    for to in range(8):
        for zz in range(4):
            cols = pl.ds((zz * 8 + to) * 128, 128)
            pltpu.make_async_copy(wout.at[:, cols], wst.at[to, zz], lsem.at[8]).start()
    doc_copy = pltpu.make_async_remote_copy(
        src_ref=doc,
        dst_ref=docm,
        send_sem=kv_ss.at[4],
        recv_sem=kv_rs.at[4],
        device_id={"seq": nxt},
        device_id_type=MESH,
    )

    @pl.when(has_next & (turn == 2))
    def _():
        doc_copy.start()

    with jax.named_scope("m_ldw"):
        ld_sn.wait()
        ld_wp.wait()
    with jax.named_scope("m_rel"):
        rel = dot(sn[...], wp[...]).astype(BF16)
    own(1)

    def share_weights():
        pltpu.make_async_copy(wst, wst, lsem.at[8]).wait()
        for n, cc in enumerate((0, 1)):
            pltpu.make_async_remote_copy(
                src_ref=wst.at[x_far * 2 + cc],
                dst_ref=via.at[n],
                send_sem=w_ss,
                recv_sem=via_rs.at[n],
                device_id={"mp": mp_of(z, x_dn, c)},
                device_id_type=MESH,
            ).start()
        for n, (xx, cc) in enumerate(peers[:5]):
            pltpu.make_async_remote_copy(
                src_ref=wst.at[xx * 2 + cc],
                dst_ref=wo.at[xc],
                send_sem=w_ss,
                recv_sem=w_rs,
                device_id={"mp": mp_of(z, xx, cc)},
                device_id_type=MESH,
            ).start()
        pltpu.make_async_copy(wst.at[xc], wo.at[xc], lsem.at[3]).start()

    def via_copy(n):
        slot = x_up * 2 + c
        return pltpu.make_async_remote_copy(
            src_ref=via.at[n],
            dst_ref=wo.at[slot],
            send_sem=via_ss,
            recv_sem=w_rs,
            device_id={"mp": mp_of(z, x_dn, n)},
            device_id_type=MESH,
        )

    def relay_weights():
        for n in (0, 1):
            arrived(via.at[n], via_rs.at[n])
            via_copy(n).start()

    def from_z(h, k):
        slot = mp_of(zo[k], x, c)
        landed(h, slot)
        push(h, slot, mp_of(z, xr, c))
        push(h, slot, mp_of(z, xl, c))
        push(h, slot, mp_of(z, x, 1 - c), True)

    def from_x(h, k):
        for xx in (x_up, x_dn):
            slot = mp_of(zo[k], xx, c)
            landed(h, slot)
            push(h, slot, mp_of(z, x, 1 - c), True)

    def from_far(h, k):
        slot = mp_of(zo[k], x_far, c)
        landed(h, slot)
        if k == 0:
            for j in (1, 2, 3):
                push(h, slot, mp_of(zo[j], x, c))
        push(h, slot, mp_of(z, x, 1 - c), True)

    def from_core(h, k):
        four = toks.at[h, pl.ds(0, 4)]
        pltpu.make_async_remote_copy(
            src_ref=four,
            dst_ref=four,
            send_sem=tok_ss.at[h],
            recv_sem=core_rs.at[h, zo[k]],
            device_id={"mp": me},
            device_id_type=MESH,
        ).wait_recv()

    def project(h, k, cc):
        slots = [mp_of(zo[k], xx, cc) for xx in range(4)]
        left = jnp.concatenate([toks[h, j] for j in slots], axis=1)
        bands = [pl.ds(pl.multiple_of(j * 128, 128), 128) for j in slots]
        right = jnp.concatenate(
            [jnp.concatenate([wv[i, band, :] for band in bands], axis=0) for i in range(3)], axis=1
        )
        return dot(left, right)

    def at(name, step, h, k):
        with jax.named_scope(f"m_{name}{h}{k}"):
            step(h, k)

    def across(h):
        at("z", from_z, h, 1)
        at("z", from_z, h, 2)
        at("far", from_far, h, 0)
        at("z", from_z, h, 3)

    def along(h, ks):
        for k in ks:
            at("x", from_x, h, k)
            if k > 0:
                at("far", from_far, h, k)

    def same(h):
        half = slice(h * 64, h * 64 + 64)
        with jax.named_scope(f"m_same{h}"):
            acc[half] = project(h, 0, c)
            for k in (1, 2, 3):
                acc[half] += project(h, k, c)

    def other(h):
        half = slice(h * 64, h * 64 + 64)
        for k in (0, 1, 2, 3):
            at("core", from_core, h, k)
            acc[half] += project(h, k, 1 - c)
        kvs[0, half] = acc[half, 128:256].astype(BF16)
        kvs[1, half] = acc[half, 256:384].astype(BF16)

    kv_copies = []
    for h in (0, 1):
        for i in (0, 1):
            kv_copies.append(
                pltpu.make_async_remote_copy(
                    src_ref=kvs.at[i, pl.ds(h * 64, 64)],
                    dst_ref=kvm.at[i, pl.ds(h * 64, 64)],
                    send_sem=kv_ss.at[h * 2 + i],
                    recv_sem=kv_rs.at[h * 2 + i],
                    device_id={"seq": nxt},
                    device_id_type=MESH,
                )
            )

    def pass_on(h):
        @pl.when(has_next & ((turn != 1) | (h == 0)))
        def _():
            for copy in kv_copies[2 * h : 2 * h + 2]:
                copy.start()

    across(0)
    across(1)

    @pl.when(turn != 2)
    def _():
        share_weights()

    along(0, (0, 1, 2, 3))
    ld_wv.wait()
    same(0)
    along(1, (0, 1))
    other(0)

    @pl.when(turn != 2)
    def _():
        pl.semaphore_wait(ready, 1)
        doc_copy.start()

    pass_on(0)
    along(1, (2, 3))

    @pl.when(turn == 2)
    def _():
        share_weights()

    same(1)
    other(1)
    pass_on(1)

    ld_cb.wait()
    ld_pb.wait()
    query = acc[:, 0:128]
    qc = (query + cbias[...]).astype(BF16)
    qp = (query + pbias[...]).astype(BF16)
    pos = pltpu.roll(dot_t(qp, rel), 129, 1, stride=1, stride_axis=0)
    scale = F32(1.0) / jnp.sqrt(F32(128.0))
    own_doc = doc[...]
    row_doc = jnp.transpose(jnp.broadcast_to(own_doc, (128, 128)))
    rows = lax.broadcasted_iota(jnp.int32, (128, 128), 0)
    cols = lax.broadcasted_iota(jnp.int32, (128, 128), 1)
    ok_own = (cols <= rows) & (row_doc == own_doc)
    s_own = (dot_t(qc, kvs[0]) + pos[:, 128:256]) * scale
    s_own = jnp.where(ok_own, s_own, F32(-1e30))
    top_own = jnp.max(s_own, axis=1, keepdims=True)

    for h in (0, 1):
        sent(toks.at[h, pl.ds(0, sends[h])], tok_ss.at[h])
    with jax.named_scope("m_via"):
        relay_weights()

    @pl.when(has_prev)
    def _():
        doc_copy.wait_recv()

    @pl.when(seq == 0)
    def _():
        docm[...] = jnp.zeros_like(docm)
        kvm[...] = jnp.zeros_like(kvm)

    ok_mem = (row_doc == docm[...]) & (seq > 0)

    with jax.named_scope("m_kv0"):

        @pl.when(has_prev)
        def _():
            for copy in kv_copies[0:3]:
                copy.wait_recv()
    s_mem = (dot_t(qc, kvm[0]) + pos[:, 0:128]) * scale
    s_mem = jnp.where(ok_mem, s_mem, F32(-1e30))
    top = jnp.maximum(top_own, jnp.max(s_mem, axis=1, keepdims=True))
    e_own = jnp.where(ok_own, jnp.exp(s_own - top), F32(0.0))
    e_mem = jnp.where(ok_mem, jnp.exp(s_mem - top), F32(0.0))
    total = jnp.sum(e_own, axis=1, keepdims=True) + jnp.sum(e_mem, axis=1, keepdims=True)
    w_own = (e_own / total).astype(BF16)
    w_mem = (e_mem / total).astype(BF16)
    with jax.named_scope("m_kv1"):

        @pl.when(has_prev)
        def _():
            kv_copies[3].wait_recv()

    rows_in = 128 // BANDS
    for half in range(BANDS):
        band = slice(half * rows_in, half * rows_in + rows_in)
        head = dot(w_own[band], kvs[1]) + dot(w_mem[band], kvm[1])
        ho[half, xc] = head.astype(BF16)
        if half > 0:
            sent(ho.at[half - 1, pl.ds(0, 7)], ho_ss.at[half - 1])
        for n, (xx, cc) in enumerate(peers):
            copy = pltpu.make_async_remote_copy(
                src_ref=ho.at[half, xc],
                dst_ref=ho.at[half, xc],
                send_sem=ho_ss.at[half],
                recv_sem=ho_rs.at[half, n // 5],
                device_id={"mp": mp_of(z, xx, cc)},
                device_id_type=MESH,
            )
            copy.start()

    def term(half, xs, zz):
        slots = [xx * 2 + cc for xx in xs for cc in (0, 1)]
        left = jnp.concatenate([ho[half, j] for j in slots], axis=1)
        right = jnp.concatenate([wo[j, zz] for j in slots], axis=0)
        return dot(left, right)

    with jax.named_scope("m_wo"):
        pltpu.make_async_copy(wo.at[xc], wo.at[xc], lsem.at[3]).wait()
        arrived(wo.at[pl.ds(0, 7)], w_rs)

    @pl.when(turn == 1)
    def _():
        for copy in kv_copies[2:4]:
            copy.start()

    for half in range(BANDS):
        with jax.named_scope(f"m_ho{half}"):
            arrived(ho.at[half, pl.ds(0, 5)], ho_rs.at[half, 0])
        for k in (3, 2, 1, 0):
            part[half, zo[k]] = term(half, (x, xr, xl), zo[k])
        with jax.named_scope(f"m_hof{half}"):
            arrived(ho.at[half, pl.ds(0, 2)], ho_rs.at[half, 1])
        for k in (3, 2, 1, 0):
            zz = zo[k]
            part[half, zz] += term(half, (x_far,), zz)
            if k > 0:
                copy = pltpu.make_async_remote_copy(
                    src_ref=part.at[half, zz],
                    dst_ref=rcv.at[half, z],
                    send_sem=p_ss.at[half],
                    recv_sem=p_rs.at[half],
                    device_id={"mp": mp_of(zz, x, c)},
                    device_id_type=MESH,
                )
                copy.start()

    sent(wst.at[pl.ds(0, 7)], w_ss)
    sent(via, via_ss)
    sent(ho.at[BANDS - 1, pl.ds(0, 7)], ho_ss.at[BANDS - 1])

    @pl.when(has_next)
    def _():
        for copy in kv_copies + [doc_copy]:
            copy.wait_send()

    for half in range(BANDS):
        with jax.named_scope(f"m_part{half}"):
            arrived(rcv.at[half, pl.ds(0, 3)], p_rs.at[half])
        result = part[half, z]
        for k in (1, 2, 3):
            result = result + rcv[half, zo[k]]
        out[half * rows_in : half * rows_in + rows_in, :] = result.astype(BF16)

    with jax.named_scope("m_send"):
        for half in range(BANDS):
            sent(part.at[half, pl.ds(0, 3)], p_ss.at[half])


def shards(tokens, w_qkv, w_pos, w_out, content_bias, position_bias, doc_ids):
    vmem = pl.BlockSpec(memory_space=pltpu.VMEM)
    hbm = pl.BlockSpec(memory_space=pltpu.HBM)
    sinus = jnp.asarray(sinus_reversed(256, 4096))
    operands = (
        tokens, w_qkv, w_pos, w_out, content_bias, position_bias, doc_ids.reshape(1, 128), sinus
    )
    operands = [pltpu.with_memory_space_constraint(a, pltpu.HBM) for a in operands]
    return pl.pallas_call(
        kernel,
        out_shape=pltpu.VMEM((128, 128), BF16),
        in_specs=[hbm] * 8,
        out_specs=vmem,
        scratch_shapes=[
            pltpu.VMEM((1, 128), F32),
            pltpu.VMEM((1, 128), F32),
            pltpu.VMEM((1, 128), jnp.int32),
            pltpu.VMEM((2, 32, 64, 128), BF16),
            pltpu.VMEM((3, 4096, 128), BF16),
            pltpu.VMEM((4096, 128), BF16),
            pltpu.VMEM((256, 4096), BF16),
            pltpu.VMEM((8, 4, 128, 128), BF16),
            pltpu.VMEM((128, 384), F32),
            pltpu.VMEM((2, 128, 128), BF16),
            pltpu.VMEM((2, 128, 128), BF16),
            pltpu.VMEM((1, 128), jnp.int32),
            pltpu.VMEM((BANDS, 8, 128 // BANDS, 128), BF16),
            pltpu.VMEM((BANDS, 4, 128 // BANDS, 128), F32),
            pltpu.VMEM((BANDS, 4, 128 // BANDS, 128), F32),
            pltpu.VMEM((8, 4, 128, 128), BF16),
            pltpu.VMEM((2, 4, 128, 128), BF16),
            pltpu.SemaphoreType.REGULAR,
            pltpu.SemaphoreType.DMA,
            pltpu.SemaphoreType.DMA((2,)),
            pltpu.SemaphoreType.DMA((11,)),
            pltpu.SemaphoreType.DMA((2,)),
            pltpu.SemaphoreType.DMA((2, 16)),
            pltpu.SemaphoreType.DMA((2, 4)),
            pltpu.SemaphoreType.DMA,
            pltpu.SemaphoreType.DMA,
            pltpu.SemaphoreType.DMA((5,)),
            pltpu.SemaphoreType.DMA((5,)),
            pltpu.SemaphoreType.DMA((BANDS,)),
            pltpu.SemaphoreType.DMA((BANDS, 2)),
            pltpu.SemaphoreType.DMA((BANDS,)),
            pltpu.SemaphoreType.DMA((BANDS,)),
        ],
        compiler_params=pltpu.CompilerParams(
            collective_id=0, has_side_effects=True, vmem_limit_bytes=20 * 1024 * 1024
        ),
        name="layer",
    )(*operands)


def solution(mesh):
    in_specs = (
        P("seq", "mp"),
        P(None, None, "mp"),
        P(None, "mp"),
        P("mp", None),
        P("mp", None),
        P("mp", None),
        P("seq"),
    )
    out_specs = P("seq", "mp")
    return jax.shard_map(shards, mesh=mesh, in_specs=in_specs, out_specs=out_specs, check_vma=False)
```
